256 devices in a mesh: region: 8 (over x, core), domain: 32 (over z, y).
Axes of the slice: x: 4, y: 4, z: 8, core: 2. Of those that a mesh axis runs over, the one named last changes fastest.
Arguments:
- midpoints: float32 [3, 131072], P(None, ('region', 'domain')), may hold values from 0 to 1, as said below
- line_vectors: float32 [3, 131072], P(None, ('region', 'domain')), may hold values from -0.046875 to 0.046875
- burgers: float32 [3, 131072], P(None, ('region', 'domain')), may hold values from -4 to 4
- destination: int32 [131072, 1], P(('region', 'domain')), may hold values from 0 to 31; in each aligned block of 512 rows (0 to 511, 512 to 1023, ...) at most 32 rows name the same one
- node_ids: int32 [2, 131072], P(None, ('region', 'domain')), may hold values from 0 to 8191
- cell_ids: int32 [131072], P(('region', 'domain')), may hold values from 0 to 127, as said below
- cell_centers: float32 [3, 1024], replicated, may hold values from 0 to 1, as said below
Outputs:
- slot_traction: float32 [3, 262144], P(None, ('region', 'domain'))
- nodal_force: float32 [3, 65536], P(None, ('region', 'domain'))
The draws below stay inside these ranges and needn't reach their ends.
Inputs may be any that keep to these rules, and one draw needn't show every extreme that they name: `destination`: among the rows of one device, no domain is named by more than 32 rows, a bound that some block reaches. `cell_ids`: region r is the slab of x from r / 8 to (r + 1) / 8 of the unit cube; its 128 cells are the boxes of a 2 x 4 x (16) grid in that slab, numbered with the last grid index fastest. `cell_centers`: each cell's center lies within its box, within a quarter of the box's width of the box's middle along each dimension. `midpoints`: each segment's midpoint lies within its cell's box.
All inputs are finite; a program needn't handle non-finite values.
Results may differ from the reference program's by a relative error of at most 0.0003.
Values sent between devices are 32-bit elements; how exact they have to be, the bound alone decides.
A program may use at most 64 MiB of HBM per device.

```python
import math
import jax
import jax.numpy as jnp
import numpy as np
from jax import lax

SEG_DEV = 512
CELLS_REG = 128
CAP = 32
SEGMENTS = 131072
CELLS = 1024
NODES_REG = 8192
N_REGION = 8
N_DOMAIN = 32


def grid_centers(key):
    index = jnp.arange(CELLS, dtype=jnp.int32)
    region = index // CELLS_REG
    local = index % CELLS_REG
    depth = CELLS_REG // 8
    grid_x = local // (4 * depth)
    grid_y = local // depth % 4
    grid_z = local % depth
    width_x = 1.0 / (2 * N_REGION)
    width_y = 0.25
    width_z = 1.0 / depth
    base = jnp.stack([((region * 2 + grid_x).astype(jnp.float32) + 0.5) * width_x, (grid_y.astype(jnp.float32) + 0.5) * width_y, (grid_z.astype(jnp.float32) + 0.5) * width_z], axis=0)
    widths = jnp.stack([jnp.full((1,), width_x, jnp.float32), jnp.full((1,), width_y, jnp.float32), jnp.full((1,), width_z, jnp.float32)], axis=0)
    jitter = jax.random.uniform(jax.random.fold_in(key, 7), (3, CELLS), jnp.float32, -0.25, 0.25) * widths
    return (base + jitter, widths)


def local_cells(key):
    return jax.random.randint(jax.random.fold_in(key, 5), (SEGMENTS,), 0, CELLS_REG, dtype=jnp.int32)


def draw_cell_centers(key, part):
    return grid_centers(key)[0]


def draw_cell_ids(key, part):
    return local_cells(key)


def draw_midpoints(key, part):
    centers, widths = grid_centers(key)
    cells = local_cells(key)
    region = jnp.arange(SEGMENTS, dtype=jnp.int32) // (SEG_DEV * N_DOMAIN)
    owner = (region * CELLS_REG + cells).astype(jnp.int32)
    offset = jax.random.uniform(jax.random.fold_in(key, 9), (3, SEGMENTS), jnp.float32, -0.24, 0.24) * widths
    return centers[:, owner] + offset


def with_ends(values, own_key, least, largest):
    place = [jax.random.randint(jax.random.fold_in(own_key, axis), (), 0, length) for axis, length in enumerate(values.shape)]
    widest = values.shape.index(max(values.shape))
    neighbour = place[:widest] + [(place[widest] + 1) % values.shape[widest]] + place[widest + 1:]
    return values.at[tuple(place)].set(least).at[tuple(neighbour)].set(largest)


def levels(stream_key, shape, cuts, low, high):
    loudness, own = 1.0, jax.random.fold_in(stream_key, 6)
    for axis_at, blocks in cuts:
        heights = jnp.exp(jax.random.uniform(jax.random.fold_in(own, axis_at), (blocks,), jnp.float32, low / len(cuts), high / len(cuts)))
        loudness = loudness * jnp.repeat(heights, shape[axis_at] // blocks).reshape([-1 if axis == axis_at else 1 for axis in range(len(shape))])
    return loudness


def shared_out(rng, own, number, rows, amount, top, bound, slope):
    ranking = jax.random.permutation(rng, amount)
    crowded, common = load_shares(amount, rows * top, bound, slope, True), load_shares(amount, rows * top, bound, slope, False)
    places = jnp.arange(amount)

    def named(sizes, offset_by):
        used = int((sizes > 0).sum())
        fixed = max(1, used // 4)
        shifted = fixed + (places - fixed + offset_by * (used - fixed)) % max(1, amount - fixed)
        return jnp.zeros((amount,), jnp.int32).at[ranking[jnp.where(places < fixed, places, shifted)]].set(jnp.asarray(sizes, jnp.int32))

    sizes = jnp.where(number % 4 == 0, named(crowded, number // 4), named(common, number - number // 4 - 1))
    mixed = jax.random.permutation(jax.random.fold_in(own, 3), amount)
    donor, sink = mixed[0:amount // 2 * 2:2], mixed[1:amount // 2 * 2:2]
    margin = jnp.minimum(sizes[donor] - 1, bound - sizes[sink]) // 2
    margin = jnp.where((donor == ranking[0]) | (sink == ranking[0]) | (sizes[sink] == 0), 0, jnp.maximum(margin, 0))
    shifted = jax.random.randint(jax.random.fold_in(own, 4), (amount // 2,), 0, 1 << 20) % (margin + 1)
    sizes = sizes.at[donor].add(-shifted).at[sink].add(shifted)
    labels = jnp.searchsorted(jnp.cumsum(sizes), jnp.arange(rows * top), side="right").astype(jnp.int32)
    table = labels.reshape(top, rows).T
    table = table[jax.random.permutation(jax.random.fold_in(own, 1), rows)]
    offset_by = jax.random.randint(jax.random.fold_in(own, 2), (rows, 1), 0, top)
    return jnp.take_along_axis(table, (jnp.arange(top)[None, :] + offset_by) % top, axis=1)


def load_shares(number_of, total, most, skew, full):
    weights = [(1 << 20) // math.isqrt(grade ** skew) + 1 for grade in range(1, number_of + 1)]
    largest = most if full else min(most, max(-(-total // number_of), total * weights[0] // sum(weights)))
    least = 1 if total - largest >= number_of - 1 else 0
    holding, surplus = [largest] + [least] * (number_of - 1), total - largest - least * (number_of - 1)
    while surplus > 0:
        candidates = [i for i in range(1, number_of) if holding[i] < largest] or [i for i in range(1, number_of) if holding[i] < most]
        pool, left = sum([weights[i] for i in candidates]), surplus
        for i in candidates:
            more = min(most - holding[i], max(1, left * weights[i] // pool), surplus)
            holding[i] = holding[i] + more
            surplus = surplus - more
    return np.array(holding)


def scatter_about(key, shape, scale, most, cuts=(), kind=jnp.bfloat16):
    gain = levels(key, shape, cuts, -0.22, 0.18) if cuts else 1.0
    values = jax.random.normal(key, shape, jnp.float32) * scale * gain
    return jnp.minimum(jnp.maximum(values, -most), most).astype(kind)


def setup_inputs(seed: int = 0) -> dict:
    streams_of = jax.random.split(jax.random.key(seed), 8)
    midpoints = draw_midpoints(jax.random.fold_in(streams_of[7], 71), 0)
    line_vectors = scatter_about(streams_of[1], (3, SEGMENTS), (SEG_DEV * N_DOMAIN) ** -0.5, 0.046875, ((1, 256),), jnp.float32)
    burgers = scatter_about(streams_of[2], (3, SEGMENTS), 1.0, 4.0, ((1, 256),), jnp.float32)
    destination_keys = jax.random.split(jax.random.fold_in(streams_of[3], 1), SEGMENTS // SEG_DEV)
    destination_turns = jax.random.permutation(jax.random.fold_in(streams_of[3], 3), SEGMENTS // SEG_DEV)
    destination = jax.vmap(lambda own, number: shared_out(jax.random.fold_in(streams_of[3], 2), own, number, SEG_DEV, N_DOMAIN, 1, CAP, 2))(destination_keys, destination_turns).reshape((SEGMENTS, 1))
    node_ids = with_ends(jax.random.randint(streams_of[4], (2, SEGMENTS), 0, NODES_REG), jax.random.fold_in(streams_of[4], 1), 0, NODES_REG - 1).astype(jnp.int32)
    cell_ids = draw_cell_ids(jax.random.fold_in(streams_of[7], 71), 0)
    cell_centers = draw_cell_centers(jax.random.fold_in(streams_of[7], 71), 0)
    return dict(midpoints=midpoints, line_vectors=line_vectors, burgers=burgers, destination=destination, node_ids=node_ids, cell_ids=cell_ids, cell_centers=cell_centers)


CORE2 = 0.01
EXACT = lax.Precision.HIGHEST

def product(left, right):
    return jnp.dot(left, right, precision=EXACT, preferred_element_type=jnp.float32)

def source_terms(m, l, b):
    count = m.shape[1]
    outer = (b[:, None, :] * l[None, :, :]).reshape(9, count)
    q = jnp.cross(b, l, axis=0)
    qm = (q[:, None, :] * m[None, :, :]).reshape(9, count)
    return (outer, jnp.concatenate([qm, q], axis=0))

def pair_block(m, outer, second, targets):
    r2 = (targets[0][None, :] - m[0][:, None]) ** 2
    r2 = r2 + (targets[1][None, :] - m[1][:, None]) ** 2
    r2 = r2 + (targets[2][None, :] - m[2][:, None]) ** 2
    g1 = 1.0 / jnp.sqrt(r2 + CORE2)
    g3 = g1 * g1 * g1
    first = product(outer, g1)
    other = product(second, g3)
    cross_part = (other[9:12][:, None, :] * targets[None, :, :]).reshape(9, targets.shape[1])
    return first + cross_part - other[0:9]

def moment_terms(m, l, b, centers):
    count = m.shape[1]
    outer = (b[:, None, :] * l[None, :, :]).reshape(9, count)
    offset = m - centers
    dipole = (outer[:, None, :] * offset[None, :, :]).reshape(27, count)
    q = jnp.cross(b, l, axis=0)
    return jnp.concatenate([outer, dipole, q], axis=0)

def far_field(moments, centers, region_centers, region, cells_reg):
    total = centers.shape[1]
    diffs = [region_centers[a][None, :] - centers[a][:, None] for a in range(3)]
    r2 = diffs[0] ** 2 + diffs[1] ** 2 + diffs[2] ** 2
    keep = (jnp.arange(total, dtype=jnp.int32) // cells_reg != region).astype(jnp.float32)
    g1 = keep[:, None] / jnp.sqrt(r2 + CORE2)
    g3 = g1 * g1 * g1
    field = product(moments[0:9], g1)
    pulls = []
    for axis_a in range(3):
        weighted = diffs[axis_a] * g3
        field = field + product(moments[9 + axis_a:36:3], weighted)
        pulls.append(product(moments[36:39], weighted))
    nterm = jnp.stack(pulls, axis=1).reshape(9, region_centers.shape[1])
    return field + nterm

def traction(stress, b):
    count = stress.shape[1]
    sigma = stress.reshape(3, 3, count)
    sym = 0.5 * (sigma + jnp.transpose(sigma, (1, 0, 2)))
    return lax.optimization_barrier(jnp.sum(sym * b[None, :, :], axis=1))

def reference(midpoints, line_vectors, burgers, destination, node_ids, cell_ids, cell_centers):
    per_region = SEG_DEV * N_DOMAIN
    total = midpoints.shape[1]
    devices = N_REGION * N_DOMAIN
    capacity = 2 * SEG_DEV // N_DOMAIN
    region_of = jnp.arange(total, dtype=jnp.int32) // per_region
    global_cell = (region_of * CELLS_REG + cell_ids).astype(jnp.int32)
    seg_centers = cell_centers[:, global_cell]
    feats = moment_terms(midpoints, line_vectors, burgers, seg_centers)
    moments = jax.ops.segment_sum(feats.T, global_cell, num_segments=CELLS_REG * N_REGION).T

    def region_traction(region):
        low = (region * per_region).astype(jnp.int32)
        m = lax.dynamic_slice_in_dim(midpoints, low, per_region, 1)
        l = lax.dynamic_slice_in_dim(line_vectors, low, per_region, 1)
        b = lax.dynamic_slice_in_dim(burgers, low, per_region, 1)
        cells = lax.dynamic_slice_in_dim(cell_ids, low, per_region, 0)
        region_centers = lax.dynamic_slice_in_dim(cell_centers, (region * CELLS_REG).astype(jnp.int32), CELLS_REG, 1)
        far = far_field(moments, cell_centers, region_centers, region, CELLS_REG)

        def add_block(total_stress, index):
            start = (index * SEG_DEV).astype(jnp.int32)
            bm = lax.dynamic_slice_in_dim(m, start, SEG_DEV, 1)
            bl = lax.dynamic_slice_in_dim(l, start, SEG_DEV, 1)
            bb = lax.dynamic_slice_in_dim(b, start, SEG_DEV, 1)
            outer, second = source_terms(bm, bl, bb)
            return (total_stress + pair_block(bm, outer, second, m), None)
        near, _ = lax.scan(add_block, jnp.zeros((9, per_region), jnp.float32), jnp.arange(N_DOMAIN, dtype=jnp.int32))
        stress = near + far[:, cells]
        return traction(stress, b)
    tractions = lax.map(region_traction, jnp.arange(N_REGION, dtype=jnp.int32))
    tractions = jnp.transpose(tractions, (1, 0, 2)).reshape(3, total)
    dest = destination[:, 0].reshape(devices, SEG_DEV)
    hot = (dest[:, :, None] == jnp.arange(N_DOMAIN, dtype=jnp.int32)[None, None, :]).astype(jnp.int32)
    rank = lax.optimization_barrier(jnp.sum(jnp.cumsum(hot, axis=1) * hot, axis=2)) - 1
    device = jnp.arange(devices, dtype=jnp.int32)[:, None]
    slot = (device // N_DOMAIN * N_DOMAIN + dest) * (2 * SEG_DEV) + device % N_DOMAIN * capacity + rank
    slot = slot.reshape(total).astype(jnp.int32)
    slot_traction = jnp.zeros((3, 2 * total), jnp.float32).at[:, slot].set(tractions)
    node_global = (region_of[None, :] * NODES_REG + node_ids).astype(jnp.int32)
    half = 0.5 * tractions
    nodal_force = jnp.zeros((3, NODES_REG * N_REGION), jnp.float32)
    nodal_force = nodal_force.at[:, node_global[0]].add(half).at[:, node_global[1]].add(half)
    return (slot_traction, nodal_force)
```

```python
import jax
import jax.numpy as jnp
from jax import lax
from jax.experimental import pallas as pl
from jax.experimental.pallas import tpu as pltpu
from jax.sharding import PartitionSpec as P

MESH = pl.DeviceIdType.MESH
F32, BF16, I32 = jnp.float32, jnp.bfloat16, jnp.int32
CORE2 = 0.01
REGIONS, DOMAINS, NZ, NY = 8, 32, 8, 4
SEG, TILE, CHUNK, LANES = 512, 256, 64, 128
CHUNKS = SEG // CHUNK


def split2(v):
    high = v.astype(BF16)
    return high, (v - high.astype(F32)).astype(BF16)


def split3(v):
    high = v.astype(BF16)
    rest = v - high.astype(F32)
    mid = rest.astype(BF16)
    return high, mid, (rest - mid.astype(F32)).astype(BF16)


def cross(b, l):
    return [b[1] * l[2] - b[2] * l[1], b[2] * l[0] - b[0] * l[2], b[0] * l[1] - b[1] * l[0]]


def rows_of(ref):
    return [ref[a : a + 1, :] for a in range(3)]


def mxu_sum(rows, steps):
    def run(*accs):
        for n, (left, right, turned) in enumerate(steps):
            unit, stage = n % 2, n // 2 % 2
            pltpu.matmul_push_rhs(right, stage, unit, transpose=turned)
            pltpu.matmul_acc_lhs(accs[unit], left, stage)
        total = pltpu.matmul_pop(accs[0])
        return total + pltpu.matmul_pop(accs[1]) if len(steps) > 1 else total

    return pl.run_scoped(run, *[pltpu.ACC(w)((rows, TILE), F32) for w in range(2)])


def padded(right):
    return jnp.concatenate([right, jnp.zeros((TILE - right.shape[0], right.shape[1]), right.dtype)], axis=0)


def dot_nt(left, right):
    tiles = [slice(k, k + TILE) for k in range(0, left.shape[1], TILE)]
    return mxu_sum(left.shape[0], [(left[:, k], padded(right[:, k]), True) for k in tiles])


def offset(k, z, y):
    i = k // NY
    odd = i % 2
    dz = odd * ((i + 1) // 2) + (1 - odd) * ((NZ - i // 2) % NZ)
    return ((z + dz) % NZ) * NY + (y + k % NY) % NY


def kernel(
    mid, lin, bur, dest, nid, cid, cen,
    slot_out, node_out,
    geo, xb, wsc, mom, my_in, mz_in, mall, msg, arrived, nodehot, rankhot, desthot,
    geo_send, geo_recv, my_send, my_recv, mz_send, mz_recv, mr_send, mr_recv, out_send, out_recv,
):
    region, dom = lax.axis_index("region"), lax.axis_index("domain")
    z, y = dom // NY, dom % NY

    barrier = pltpu.get_barrier_semaphore()

    def greet_domain(k, c):
        pl.semaphore_signal(barrier, inc=1, device_id=(region, (dom + k) % DOMAINS), device_id_type=MESH)
        return c

    def greet_region(k, c):
        pl.semaphore_signal(barrier, inc=1, device_id=((region + k) % REGIONS, dom), device_id_type=MESH)
        return c

    lax.fori_loop(1, DOMAINS, greet_domain, 0)
    lax.fori_loop(1, REGIONS, greet_region, 0)

    def empty(*accs):
        for acc in accs:
            pltpu.matmul_pop(acc)

    pl.run_scoped(empty, *[pltpu.ACC(w)((SEG, TILE), F32) for w in range(2)])

    middle = [(region.astype(F32) + 0.5) / REGIONS, 0.5, 0.5]
    m = [mid[a : a + 1, :] - middle[a] for a in range(3)]
    l, b = rows_of(lin), rows_of(bur)
    for c, row in enumerate(m + l + b):
        for j in range(4):
            geo[0, 4 * c + j : 4 * c + j + 1, :] = row[:, j * LANES : (j + 1) * LANES]
    for j in range(4):
        geo[0, 36 + j : 37 + j, :] = jnp.zeros((1, LANES), F32)

    outer = [b[i] * l[j] for i in range(3) for j in range(3)]
    q = cross(b, l)
    zero = jnp.zeros((1, SEG), F32)
    feats = outer + [outer[k] * m[a] for a in range(3) for k in range(9)]
    feats = jnp.concatenate(feats + q + [zero], axis=0)
    cell_hot = (lax.broadcasted_iota(I32, (LANES, SEG), 0) == cid[...]).astype(F32).astype(BF16)
    feats = [jnp.concatenate([part, jnp.zeros((8, SEG), BF16)], axis=0) for part in split3(feats)]
    parts = dot_nt(jnp.concatenate(feats, axis=0), cell_hot)[:, 0:LANES]
    mom[...] = parts[0:40] + parts[48:88] + parts[96:136]

    pl.semaphore_wait(barrier, DOMAINS - 1 + REGIONS - 1)

    def y_copy(k):
        return pltpu.make_async_remote_copy(
            src_ref=mom, dst_ref=my_in.at[k], send_sem=my_send.at[k], recv_sem=my_recv.at[k],
            device_id=(region, z * NY + (y + k) % NY), device_id_type=MESH)

    def geo_copy(k):
        return pltpu.make_async_remote_copy(
            src_ref=geo.at[0], dst_ref=geo.at[k], send_sem=geo_send.at[k], recv_sem=geo_recv.at[k],
            device_id=(region, offset(k, z, y)), device_id_type=MESH)

    def z_copy(k):
        return pltpu.make_async_remote_copy(
            src_ref=mz_in.at[0], dst_ref=mz_in.at[k], send_sem=mz_send.at[k], recv_sem=mz_recv.at[k],
            device_id=(region, ((z + k) % NZ) * NY + y), device_id_type=MESH)

    def r_copy(k):
        return pltpu.make_async_remote_copy(
            src_ref=mall.at[0], dst_ref=mall.at[k], send_sem=mr_send.at[k], recv_sem=mr_recv.at[k],
            device_id=((region + k) % REGIONS, dom), device_id_type=MESH)

    def start(copy):
        def run(k, c):
            copy(k).start()
            return c

        return run

    for k in range(1, NY):
        y_copy(k).start()
    lax.fori_loop(1, DOMAINS, start(geo_copy), 0)

    d = dest[...]
    hot = (lax.broadcasted_iota(I32, (DOMAINS, SEG), 0) == d).astype(F32)
    upper = lax.broadcasted_iota(I32, (TILE, TILE), 0) < lax.broadcasted_iota(I32, (TILE, TILE), 1)
    upper = upper.astype(F32).astype(BF16)
    first, second = hot[:, 0:TILE].astype(BF16), hot[:, TILE:SEG].astype(BF16)
    ones = jnp.ones((TILE, TILE), BF16)
    before = jnp.concatenate(
        [mxu_sum(DOMAINS, [(first, upper, False)]), mxu_sum(DOMAINS, [(second, upper, False), (first, ones, False)])], axis=1
    )
    rank = jnp.sum(before * hot, axis=0, keepdims=True)
    desthot[...] = hot
    rankhot[...] = (lax.broadcasted_iota(I32, (DOMAINS, SEG), 0).astype(F32) == rank).astype(F32).astype(BF16)
    for e in range(2):
        low = nid[e : e + 1, :] & (LANES - 1)
        nodehot[:, e * SEG : (e + 1) * SEG] = (lax.broadcasted_iota(I32, (LANES, SEG), 0) == low).astype(F32).astype(BF16)

    own = jnp.concatenate([-2.0 * m[a] for a in range(3)] + [m[0] * m[0] + m[1] * m[1] + m[2] * m[2] + CORE2] + [zero] * 4, axis=0)
    columns = jnp.transpose(own)
    for a in range(4):
        xb[a] = jnp.broadcast_to(columns[:, a : a + 1], (SEG, LANES))
    wsc[...] = jnp.zeros_like(wsc)

    def pairs(*accs):
        acc1, acc3 = accs[:CHUNKS], accs[CHUNKS:]
        blank = jnp.zeros((TILE - 32, TILE), BF16)

        def block(k):
            v = [geo[k, 4 * c : 4 * c + 4, :] for c in range(9)]
            vm, vl, vb = v[0:3], v[3:6], v[6:9]
            vq = cross(vb, vl)
            for i in range(3):
                for j in range(3):
                    at = 4 * (3 * i + j)
                    wsc[0, at : at + 4, :] = vb[i] * vl[j]
                    wsc[1, at : at + 4, :] = vq[i] * vm[j]
                wsc[1, 36 + 4 * i : 40 + 4 * i, :] = vq[i]
            for t in range(2):
                for w in range(2):
                    wide = jnp.concatenate([wsc[w, pl.ds(2 * t + u, 16, stride=4), :] for u in range(2)], axis=1)
                    high, low = split2(wide)
                    pltpu.matmul_push_rhs(jnp.concatenate([high, low, blank], axis=0), 0, w, transpose=True)
                s = [
                    jnp.concatenate([geo[k, 4 * a + 2 * t + u : 4 * a + 2 * t + u + 1, :] for u in range(2)], axis=1)
                    for a in range(3)
                ]
                s2 = s[0] * s[0] + s[1] * s[1] + s[2] * s[2]
                for c in range(CHUNKS):
                    x = [jnp.concatenate([xb[a, c * CHUNK : (c + 1) * CHUNK, :]] * 2, axis=1) for a in range(4)]
                    g1 = lax.rsqrt((x[3] + s2) + x[0] * s[0] + x[1] * s[1] + x[2] * s[2])
                    h1, l1 = split2(g1)
                    h3, l3 = split2(g1 * g1 * g1)
                    first = 0 if c == 0 else None
                    pltpu.matmul_acc_lhs(acc1[c], h1, first)
                    pltpu.matmul_acc_lhs(acc3[c], h3, first)
                    pltpu.matmul_acc_lhs(acc1[c], l1)
                    pltpu.matmul_acc_lhs(acc3[c], l3)

        def arrived_block(k, carry):
            geo_copy(k).wait_recv()
            block(k)
            return carry

        block(0)
        for k in range(1, NY):
            y_copy(k).wait_recv()
        mz_in[0] = mom[...] + my_in[1] + my_in[2] + my_in[3]
        for k in range(1, NZ):
            z_copy(k).start()
        lax.fori_loop(1, 10, arrived_block, 0)
        for k in range(1, NZ):
            z_copy(k).wait_recv()
        total = mz_in[0]
        for k in range(1, NZ):
            total = total + mz_in[k]
        center = [cen[a : a + 1, pl.ds(pl.multiple_of(region * LANES, LANES), LANES)] - middle[a] for a in range(3)]
        mall[0, 0:9, :] = total[0:9]
        for a in range(3):
            for k in range(9):
                at = 9 + 9 * a + k
                value = total[at : at + 1] - center[a] * total[k : k + 1]
                if k % 3 == a:
                    value = value + total[36 + k // 3 : 37 + k // 3]
                mall[0, at : at + 1, :] = value
        mall[0, 36:40, :] = jnp.zeros((4, LANES), F32)
        for k in range(1, REGIONS):
            r_copy(k).start()
        lax.fori_loop(10, DOMAINS, arrived_block, 0)
        for c in range(CHUNKS):
            one, three = pltpu.matmul_pop(acc1[c]), pltpu.matmul_pop(acc3[c])
            xb[0, c * CHUNK : (c + 1) * CHUNK, :] = one[:, 0:LANES]
            xb[1, c * CHUNK : (c + 1) * CHUNK, :] = three[:, 0:LANES]

    pl.run_scoped(pairs, *[pltpu.ACC(w)((CHUNK, TILE), F32) for w in range(2) for _ in range(CHUNKS)])

    for k in range(1, REGIONS):
        r_copy(k).wait_recv()
    at = pl.ds(pl.multiple_of(region * LANES, LANES), LANES)
    target = jnp.transpose(jnp.concatenate([cen[0:3, at], jnp.zeros((5, LANES), F32)], axis=0))
    target = [jnp.broadcast_to(target[:, a : a + 1], (LANES, LANES)) for a in range(3)]
    weights, kernels = [], []
    for k in range(1, REGIONS):
        source = pl.ds(pl.multiple_of(((region + REGIONS - k) % REGIONS) * LANES, LANES), LANES)
        diff = [target[a] - cen[a : a + 1, source] for a in range(3)]
        g1 = lax.rsqrt(diff[0] * diff[0] + diff[1] * diff[1] + diff[2] * diff[2] + CORE2)
        g3 = g1 * g1 * g1
        total = mall[k]
        for p, part in enumerate([g1] + [diff[a] * g3 for a in range(3)]):
            high, low = split2(part)
            wh, wl = split2(jnp.concatenate([total[9 * p : 9 * p + 9], jnp.zeros((7, LANES), F32)], axis=0))
            both = jnp.concatenate([wh, wl], axis=0)
            kernels += [high, low]
            weights += [both, both]
    far = dot_nt(jnp.concatenate(weights, axis=1), jnp.concatenate(kernels, axis=1))
    far = split3(far[0:16, 0:LANES] + far[16:32, 0:LANES])
    cell_hot = (lax.broadcasted_iota(I32, (TILE, SEG), 0) % LANES == cid[...]).astype(F32).astype(BF16)
    pair = [jnp.concatenate(far[0:2], axis=1), jnp.concatenate([far[2], jnp.zeros_like(far[2])], axis=1)]
    far = jnp.concatenate(
        [mxu_sum(16, [(left, cell_hot[:, k : k + TILE], False) for left in pair]) for k in (0, TILE)], axis=1
    )

    one, three = jnp.transpose(xb[0]), jnp.transpose(xb[1])
    one = one[0:16] + one[16:32]
    three = three[0:16] + three[16:32]
    x = [mid[a : a + 1, :] - middle[a] for a in range(3)]
    b = rows_of(bur)
    stress = [
        one[k : k + 1] + far[k : k + 1] + three[9 + k // 3 : 10 + k // 3] * x[k % 3] - three[k : k + 1] for k in range(9)
    ]
    force = []
    for i in range(3):
        total = zero
        for j in range(3):
            total = total + 0.5 * (stress[3 * i + j] + stress[3 * j + i]) * b[j]
        force.append(total)

    halves = [0.5 * f for f in force]
    table = jnp.concatenate([halves[0]] * 2 + [halves[1]] * 2 + [halves[2]] * 2 + [zero] * 2, axis=0)
    table_high = table.astype(BF16).astype(F32)
    table_low = table - table_high
    sub = lax.broadcasted_iota(I32, (8, SEG), 0) % 2
    lefts = []
    for e in range(2):
        row = (nid[e : e + 1, :] // LANES) - sub
        hits = [row == 2 * owner for owner in range(DOMAINS)]
        for part in (table_high, table_low):
            lefts.append(jnp.concatenate([jnp.where(hit, part, 0.0) for hit in hits], axis=0).astype(BF16))
    rights = [nodehot[:, e * SEG : (e + 1) * SEG] for e in (0, 0, 1, 1)]
    nodes = dot_nt(jnp.concatenate(lefts, axis=1), jnp.concatenate(rights, axis=1))
    hot = desthot[...]
    left = [part for c in range(3) for part in split3(hot * force[c])]
    part = dot_nt(jnp.concatenate(left, axis=0), rankhot[...])[:, 0:32]
    slots = [part[96 * c : 96 * c + 32] + part[96 * c + 32 : 96 * c + 64] + part[96 * c + 64 : 96 * c + 96] for c in range(3)]
    slots = jnp.concatenate(slots + [jnp.zeros((DOMAINS, 32), F32)], axis=1)
    msg[...] = nodes[:, 0:LANES]
    msg[pl.ds(6, DOMAINS, stride=8), :] = slots

    def out_copy(k):
        peer = (dom + k) % DOMAINS
        return pltpu.make_async_remote_copy(
            src_ref=msg.at[pl.ds(pl.multiple_of(8 * peer, 8), 8), :],
            dst_ref=arrived.at[pl.ds(pl.multiple_of(8 * dom, 8), 8), :],
            send_sem=out_send.at[k], recv_sem=out_recv.at[k],
            device_id=(region, peer), device_id_type=MESH)

    lax.fori_loop(1, DOMAINS, start(out_copy), 0)
    mine = pl.ds(pl.multiple_of(8 * dom, 8), 8)
    arrived[mine, :] = msg[mine, :]

    def received(k, c):
        out_copy(k).wait_recv()
        return c

    lax.fori_loop(1, DOMAINS, received, 0)
    total = arrived[0:8, :]
    for s in range(1, DOMAINS):
        total = total + arrived[8 * s : 8 * s + 8, :]
    for c in range(3):
        for h in range(2):
            node_out[c : c + 1, h * LANES : (h + 1) * LANES] = total[2 * c + h : 2 * c + h + 1]
    quarter = lax.broadcasted_iota(I32, (8, LANES), 1) // 32
    four = [arrived[pl.ds(6 + 8 * a, 8, stride=32), :] for a in range(4)]
    for c in range(3):
        line = jnp.zeros((8, LANES), F32)
        for a in range(4):
            turn = (32 * (a - c)) % LANES
            line = jnp.where(quarter == a, pltpu.roll(four[a], turn, 1) if turn else four[a], line)
        for j in range(8):
            slot_out[c : c + 1, j * LANES : (j + 1) * LANES] = line[j : j + 1]

    for copy, count in ((y_copy, NY), (geo_copy, DOMAINS), (z_copy, NZ), (r_copy, REGIONS), (out_copy, DOMAINS)):

        def sent(k, c, copy=copy):
            copy(k).wait_send()
            return c

        lax.fori_loop(1, count, sent, 0)


def body(midpoints, line_vectors, burgers, destination, node_ids, cell_ids, cell_centers):
    vmem = pl.BlockSpec(memory_space=pltpu.VMEM)
    dma = pltpu.SemaphoreType.DMA
    return pl.pallas_call(
        kernel,
        out_shape=(jax.ShapeDtypeStruct((3, 2 * SEG), F32), jax.ShapeDtypeStruct((3, 256), F32)),
        in_specs=[vmem] * 7,
        out_specs=(vmem, vmem),
        scratch_shapes=[
            pltpu.VMEM((DOMAINS, 40, LANES), F32),
            pltpu.VMEM((4, SEG, LANES), F32),
            pltpu.VMEM((2, 64, LANES), F32),
            pltpu.VMEM((40, LANES), F32),
            pltpu.VMEM((NY, 40, LANES), F32),
            pltpu.VMEM((NZ, 40, LANES), F32),
            pltpu.VMEM((REGIONS, 40, LANES), F32),
            pltpu.VMEM((DOMAINS * 8, LANES), F32),
            pltpu.VMEM((DOMAINS * 8, LANES), F32),
            pltpu.VMEM((LANES, 2 * SEG), BF16),
            pltpu.VMEM((DOMAINS, SEG), BF16),
            pltpu.VMEM((DOMAINS, SEG), F32),
            dma((DOMAINS,)), dma((DOMAINS,)), dma((NY,)), dma((NY,)), dma((NZ,)), dma((NZ,)),
            dma((REGIONS,)), dma((REGIONS,)), dma((DOMAINS,)), dma((DOMAINS,)),
        ],
        compiler_params=pltpu.CompilerParams(
            collective_id=0, has_side_effects=True, vmem_limit_bytes=32 << 20
        ),
    )(
        midpoints, line_vectors, burgers, destination.reshape(1, SEG), node_ids, cell_ids.reshape(1, SEG), cell_centers
    )


def solution(mesh):
    both = ("region", "domain")

    def program(*args):
        with jax.sharding.use_abstract_mesh(mesh.abstract_mesh):
            return jax.shard_map(
                body,
                mesh=mesh,
                in_specs=(P(None, both), P(None, both), P(None, both), P(both, None), P(None, both), P(both), P()),
                out_specs=(P(None, both), P(None, both)),
                check_vma=False,
            )(*args)

    return program
```

```python
import jax
import jax.numpy as jnp
from jax import lax
from jax.experimental import pallas as pl
from jax.experimental.pallas import tpu as pltpu
from jax.sharding import PartitionSpec as P

MESH = pl.DeviceIdType.MESH
F32, BF16, I32 = jnp.float32, jnp.bfloat16, jnp.int32
CORE2 = 0.01
REGIONS, DOMAINS, NZ, NY = 8, 32, 8, 4
SEG, TILE, CHUNK, LANES = 512, 256, 64, 128
CHUNKS = SEG // CHUNK


def split2(v):
    high = v.astype(BF16)
    return high, (v - high.astype(F32)).astype(BF16)


def split3(v):
    high = v.astype(BF16)
    rest = v - high.astype(F32)
    mid = rest.astype(BF16)
    return high, mid, (rest - mid.astype(F32)).astype(BF16)


def cross(b, l):
    return [b[1] * l[2] - b[2] * l[1], b[2] * l[0] - b[0] * l[2], b[0] * l[1] - b[1] * l[0]]


def rows_of(ref):
    return [ref[a : a + 1, :] for a in range(3)]


def mxu_sum(rows, steps):
    def run(*accs):
        for n, (left, right, turned) in enumerate(steps):
            unit, stage = n % 2, n // 2 % 2
            pltpu.matmul_push_rhs(right, stage, unit, transpose=turned)
            pltpu.matmul_acc_lhs(accs[unit], left, stage)
        total = pltpu.matmul_pop(accs[0])
        return total + pltpu.matmul_pop(accs[1]) if len(steps) > 1 else total

    return pl.run_scoped(run, *[pltpu.ACC(w)((rows, TILE), F32) for w in range(2)])


def padded(right):
    return jnp.concatenate([right, jnp.zeros((TILE - right.shape[0], right.shape[1]), right.dtype)], axis=0)


def dot_nt(left, right):
    tiles = [slice(k, k + TILE) for k in range(0, left.shape[1], TILE)]
    return mxu_sum(left.shape[0], [(left[:, k], padded(right[:, k]), True) for k in tiles])


def offset(k, z, y):
    i = k // NY
    odd = i % 2
    dz = odd * ((i + 1) // 2) + (1 - odd) * ((NZ - i // 2) % NZ)
    return ((z + dz) % NZ) * NY + (y + k % NY) % NY


def kernel(
    mid_in, lin_in, bur_in, dest_in, nid_in, cid_in, cen_in,
    slot_out, node_out,
    mid, lin, bur, dest, nid, cid, cen, in_sem, kern,
    geo, xb, wsc, mom, my_in, mz_in, mall, msg, arrived, nodehot, rankhot, desthot,
    geo_send, geo_recv, my_send, my_recv, mz_send, mz_recv, mr_send, mr_recv, out_send, out_recv,
):
    region, dom = lax.axis_index("region"), lax.axis_index("domain")
    z, y = dom // NY, dom % NY

    barrier = pltpu.get_barrier_semaphore()

    def greet_domain(k, c):
        pl.semaphore_signal(barrier, inc=1, device_id=(region, (dom + k) % DOMAINS), device_id_type=MESH)
        return c

    def greet_region(k, c):
        pl.semaphore_signal(barrier, inc=1, device_id=((region + k) % REGIONS, dom), device_id_type=MESH)
        return c

    lax.fori_loop(1, DOMAINS, greet_domain, 0)
    lax.fori_loop(1, REGIONS, greet_region, 0)

    pairs_in = zip((mid_in, lin_in, bur_in, dest_in, nid_in, cid_in, cen_in), (mid, lin, bur, dest, nid, cid, cen))
    loads = [pltpu.make_async_copy(there, here, in_sem.at[n]) for n, (there, here) in enumerate(pairs_in)]
    for load in loads:
        load.start()

    def empty(*accs):
        for acc in accs:
            pltpu.matmul_pop(acc)

    pl.run_scoped(empty, *[pltpu.ACC(w)((SEG, TILE), F32) for w in range(2)])

    for load in loads:
        load.wait()

    middle = [(region.astype(F32) + 0.5) / REGIONS, 0.5, 0.5]
    m = [mid[a : a + 1, :] - middle[a] for a in range(3)]
    l, b = rows_of(lin), rows_of(bur)
    for c, row in enumerate(m + l + b):
        for j in range(4):
            geo[0, 4 * c + j : 4 * c + j + 1, :] = row[:, j * LANES : (j + 1) * LANES]
    for j in range(4):
        geo[0, 36 + j : 37 + j, :] = jnp.zeros((1, LANES), F32)

    outer = [b[i] * l[j] for i in range(3) for j in range(3)]
    q = cross(b, l)
    zero = jnp.zeros((1, SEG), F32)
    feats = outer + [outer[k] * m[a] for a in range(3) for k in range(9)]
    feats = jnp.concatenate(feats + q + [zero], axis=0)
    cell_hot = (lax.broadcasted_iota(I32, (LANES, SEG), 0) == cid[...]).astype(F32).astype(BF16)
    feats = [jnp.concatenate([part, jnp.zeros((8, SEG), BF16)], axis=0) for part in split3(feats)]
    parts = dot_nt(jnp.concatenate(feats, axis=0), cell_hot)[:, 0:LANES]
    mom[...] = parts[0:40] + parts[48:88] + parts[96:136]

    def y_copy(k):
        return pltpu.make_async_remote_copy(
            src_ref=mom, dst_ref=my_in.at[k], send_sem=my_send.at[k], recv_sem=my_recv.at[k],
            device_id=(region, z * NY + (y + k) % NY), device_id_type=MESH)

    def geo_copy(k):
        return pltpu.make_async_remote_copy(
            src_ref=geo.at[0], dst_ref=geo.at[k], send_sem=geo_send.at[k], recv_sem=geo_recv.at[k],
            device_id=(region, offset(k, z, y)), device_id_type=MESH)

    def z_copy(k):
        return pltpu.make_async_remote_copy(
            src_ref=mz_in.at[0], dst_ref=mz_in.at[k], send_sem=mz_send.at[k], recv_sem=mz_recv.at[k],
            device_id=(region, ((z + k) % NZ) * NY + y), device_id_type=MESH)

    def r_copy(k):
        return pltpu.make_async_remote_copy(
            src_ref=mall.at[0], dst_ref=mall.at[k], send_sem=mr_send.at[k], recv_sem=mr_recv.at[k],
            device_id=((region + k) % REGIONS, dom), device_id_type=MESH)

    def start(copy):
        def run(k, c):
            copy(k).start()
            return c

        return run

    d = dest[...]
    hot = (lax.broadcasted_iota(I32, (DOMAINS, SEG), 0) == d).astype(F32)
    upper = lax.broadcasted_iota(I32, (TILE, TILE), 0) < lax.broadcasted_iota(I32, (TILE, TILE), 1)
    upper = upper.astype(F32).astype(BF16)
    first, second = hot[:, 0:TILE].astype(BF16), hot[:, TILE:SEG].astype(BF16)
    ones = jnp.ones((TILE, TILE), BF16)
    before = jnp.concatenate(
        [mxu_sum(DOMAINS, [(first, upper, False)]), mxu_sum(DOMAINS, [(second, upper, False), (first, ones, False)])], axis=1
    )
    rank = jnp.sum(before * hot, axis=0, keepdims=True)
    desthot[...] = hot
    rankhot[...] = (lax.broadcasted_iota(I32, (DOMAINS, SEG), 0).astype(F32) == rank).astype(F32).astype(BF16)
    for e in range(2):
        low = nid[e : e + 1, :] & (LANES - 1)
        nodehot[:, e * SEG : (e + 1) * SEG] = (lax.broadcasted_iota(I32, (LANES, SEG), 0) == low).astype(F32).astype(BF16)

    own = jnp.concatenate([-2.0 * m[a] for a in range(3)] + [m[0] * m[0] + m[1] * m[1] + m[2] * m[2] + CORE2] + [zero] * 4, axis=0)
    columns = jnp.transpose(own)
    for a in range(4):
        xb[a] = jnp.broadcast_to(columns[:, a : a + 1], (SEG, LANES))
    wsc[...] = jnp.zeros_like(wsc)

    at = pl.ds(pl.multiple_of(region * LANES, LANES), LANES)
    target = jnp.transpose(jnp.concatenate([cen[0:3, at], jnp.zeros((5, LANES), F32)], axis=0))
    target = [jnp.broadcast_to(target[:, a : a + 1], (LANES, LANES)) for a in range(3)]
    for k in range(1, REGIONS):
        source = pl.ds(pl.multiple_of(((region + REGIONS - k) % REGIONS) * LANES, LANES), LANES)
        diff = [target[a] - cen[a : a + 1, source] for a in range(3)]
        g1 = lax.rsqrt(diff[0] * diff[0] + diff[1] * diff[1] + diff[2] * diff[2] + CORE2)
        g3 = g1 * g1 * g1
        for p, part in enumerate([g1] + [diff[a] * g3 for a in range(3)]):
            kern[4 * (k - 1) + p] = jnp.concatenate(split2(part), axis=1)

    def pairs(*accs):
        acc1, acc3 = accs[:CHUNKS], accs[CHUNKS:]
        blank = jnp.zeros((TILE - 32, TILE), BF16)

        def prepare(k, slot):
            v = [geo[k, 4 * c : 4 * c + 4, :] for c in range(9)]
            vm, vl, vb = v[0:3], v[3:6], v[6:9]
            vq = cross(vb, vl)
            for i in range(3):
                for j in range(3):
                    at = 4 * (3 * i + j)
                    wsc[slot, 0, at : at + 4, :] = vb[i] * vl[j]
                    wsc[slot, 1, at : at + 4, :] = vq[i] * vm[j]
                wsc[slot, 1, 36 + 4 * i : 40 + 4 * i, :] = vq[i]

        def push(slot, t):
            for w in range(2):
                wide = jnp.concatenate([wsc[slot, w, pl.ds(2 * t + u, 16, stride=4), :] for u in range(2)], axis=1)
                high, low = split2(wide)
                pltpu.matmul_push_rhs(jnp.concatenate([high, low, blank], axis=0), t, w, transpose=True)

        def stream(k, t):
            s = [
                jnp.concatenate([geo[k, 4 * a + 2 * t + u : 4 * a + 2 * t + u + 1, :] for u in range(2)], axis=1)
                for a in range(3)
            ]
            s2 = s[0] * s[0] + s[1] * s[1] + s[2] * s[2]
            for c in range(CHUNKS):
                x = [jnp.concatenate([xb[a, c * CHUNK : (c + 1) * CHUNK, :]] * 2, axis=1) for a in range(4)]
                g1 = lax.rsqrt((x[3] + s2) + x[0] * s[0] + x[1] * s[1] + x[2] * s[2])
                h1, l1 = split2(g1)
                h3, l3 = split2(g1 * g1 * g1)
                first = t if c == 0 else None
                pltpu.matmul_acc_lhs(acc1[c], h1, first)
                pltpu.matmul_acc_lhs(acc3[c], h3, first)
                pltpu.matmul_acc_lhs(acc1[c], l1)
                pltpu.matmul_acc_lhs(acc3[c], l3)

        def block(k, carry):
            push(k % 2, 1)
            stream(k, 0)
            geo_copy(k + 1).wait_recv()
            prepare(k + 1, (k + 1) % 2)
            push((k + 1) % 2, 0)
            stream(k, 1)
            return carry

        prepare(0, 0)
        push(0, 0)
        push(0, 1)
        stream(0, 0)
        stream(0, 1)

        pl.semaphore_wait(barrier, DOMAINS - 1 + REGIONS - 1)
        for k in range(1, NY):
            y_copy(k).start()
        lax.fori_loop(1, DOMAINS, start(geo_copy), 0)
        geo_copy(1).wait_recv()
        prepare(1, 1)
        push(1, 0)
        lax.fori_loop(1, 8, block, 0)
        for k in range(1, NY):
            y_copy(k).wait_recv()
        mz_in[0] = mom[...] + my_in[1] + my_in[2] + my_in[3]
        for k in range(1, NZ):
            z_copy(k).start()
        lax.fori_loop(8, 17, block, 0)
        for k in range(1, NZ):
            z_copy(k).wait_recv()
        total = mz_in[0]
        for k in range(1, NZ):
            total = total + mz_in[k]
        center = [cen[a : a + 1, pl.ds(pl.multiple_of(region * LANES, LANES), LANES)] - middle[a] for a in range(3)]
        mall[0, 0:9, :] = total[0:9]
        for a in range(3):
            for k in range(9):
                at = 9 + 9 * a + k
                value = total[at : at + 1] - center[a] * total[k : k + 1]
                if k % 3 == a:
                    value = value + total[36 + k // 3 : 37 + k // 3]
                mall[0, at : at + 1, :] = value
        mall[0, 36:40, :] = jnp.zeros((4, LANES), F32)
        for k in range(1, REGIONS):
            r_copy(k).start()
        lax.fori_loop(17, DOMAINS - 1, block, 0)
        push((DOMAINS - 1) % 2, 1)
        stream(DOMAINS - 1, 0)
        stream(DOMAINS - 1, 1)
        for c in range(CHUNKS):
            one, three = pltpu.matmul_pop(acc1[c]), pltpu.matmul_pop(acc3[c])
            xb[0, c * CHUNK : (c + 1) * CHUNK, :] = one[:, 0:LANES]
            xb[1, c * CHUNK : (c + 1) * CHUNK, :] = three[:, 0:LANES]

    pl.run_scoped(pairs, *[pltpu.ACC(w)((CHUNK, TILE), F32) for w in range(2) for _ in range(CHUNKS)])

    for k in range(1, REGIONS):
        r_copy(k).wait_recv()
    steps = []
    for k in range(1, REGIONS):
        total = mall[k]
        for p in range(4):
            wh, wl = split2(jnp.concatenate([total[9 * p : 9 * p + 9], jnp.zeros((7, LANES), F32)], axis=0))
            both = jnp.concatenate([wh, wl], axis=0)
            steps.append((jnp.concatenate([both, both], axis=1), padded(kern[4 * (k - 1) + p]), True))
    far = mxu_sum(32, steps)
    far = split3(far[0:16, 0:LANES] + far[16:32, 0:LANES])
    cell_hot = (lax.broadcasted_iota(I32, (TILE, SEG), 0) % LANES == cid[...]).astype(F32).astype(BF16)
    pair = [jnp.concatenate(far[0:2], axis=1), jnp.concatenate([far[2], jnp.zeros_like(far[2])], axis=1)]
    far = jnp.concatenate(
        [mxu_sum(16, [(left, cell_hot[:, k : k + TILE], False) for left in pair]) for k in (0, TILE)], axis=1
    )

    one, three = jnp.transpose(xb[0]), jnp.transpose(xb[1])
    one = one[0:16] + one[16:32]
    three = three[0:16] + three[16:32]
    x = [mid[a : a + 1, :] - middle[a] for a in range(3)]
    b = rows_of(bur)
    stress = [
        one[k : k + 1] + far[k : k + 1] + three[9 + k // 3 : 10 + k // 3] * x[k % 3] - three[k : k + 1] for k in range(9)
    ]
    force = []
    for i in range(3):
        total = zero
        for j in range(3):
            total = total + 0.5 * (stress[3 * i + j] + stress[3 * j + i]) * b[j]
        force.append(total)

    halves = [0.5 * f for f in force]
    table = jnp.concatenate([halves[0]] * 2 + [halves[1]] * 2 + [halves[2]] * 2 + [zero] * 2, axis=0)
    table_high = table.astype(BF16).astype(F32)
    table_low = table - table_high
    sub = lax.broadcasted_iota(I32, (8, SEG), 0) % 2
    lefts = []
    for e in range(2):
        row = (nid[e : e + 1, :] // LANES) - sub
        hits = [row == 2 * owner for owner in range(DOMAINS)]
        for part in (table_high, table_low):
            lefts.append(jnp.concatenate([jnp.where(hit, part, 0.0) for hit in hits], axis=0).astype(BF16))
    rights = [nodehot[:, e * SEG : (e + 1) * SEG] for e in (0, 0, 1, 1)]
    nodes = dot_nt(jnp.concatenate(lefts, axis=1), jnp.concatenate(rights, axis=1))
    hot = desthot[...]
    left = [part for c in range(3) for part in split3(hot * force[c])]
    part = dot_nt(jnp.concatenate(left, axis=0), rankhot[...])[:, 0:32]
    slots = [part[96 * c : 96 * c + 32] + part[96 * c + 32 : 96 * c + 64] + part[96 * c + 64 : 96 * c + 96] for c in range(3)]
    slots = jnp.concatenate(slots + [jnp.zeros((DOMAINS, 32), F32)], axis=1)
    msg[...] = nodes[:, 0:LANES]
    msg[pl.ds(6, DOMAINS, stride=8), :] = slots

    def out_copy(k):
        peer = (dom + k) % DOMAINS
        return pltpu.make_async_remote_copy(
            src_ref=msg.at[pl.ds(pl.multiple_of(8 * peer, 8), 8), :],
            dst_ref=arrived.at[pl.ds(pl.multiple_of(8 * dom, 8), 8), :],
            send_sem=out_send.at[k], recv_sem=out_recv.at[k],
            device_id=(region, peer), device_id_type=MESH)

    lax.fori_loop(1, DOMAINS, start(out_copy), 0)
    mine = pl.ds(pl.multiple_of(8 * dom, 8), 8)
    arrived[mine, :] = msg[mine, :]

    def received(k, c):
        out_copy(k).wait_recv()
        return c

    lax.fori_loop(1, DOMAINS, received, 0)
    total = arrived[0:8, :]
    for s in range(1, DOMAINS):
        total = total + arrived[8 * s : 8 * s + 8, :]
    for c in range(3):
        for h in range(2):
            node_out[c : c + 1, h * LANES : (h + 1) * LANES] = total[2 * c + h : 2 * c + h + 1]
    quarter = lax.broadcasted_iota(I32, (8, LANES), 1) // 32
    four = [arrived[pl.ds(6 + 8 * a, 8, stride=32), :] for a in range(4)]
    for c in range(3):
        line = jnp.zeros((8, LANES), F32)
        for a in range(4):
            turn = (32 * (a - c)) % LANES
            line = jnp.where(quarter == a, pltpu.roll(four[a], turn, 1) if turn else four[a], line)
        for j in range(8):
            slot_out[c : c + 1, j * LANES : (j + 1) * LANES] = line[j : j + 1]

    for copy, count in ((y_copy, NY), (geo_copy, DOMAINS), (z_copy, NZ), (r_copy, REGIONS), (out_copy, DOMAINS)):

        def sent(k, c, copy=copy):
            copy(k).wait_send()
            return c

        lax.fori_loop(1, count, sent, 0)


def body(midpoints, line_vectors, burgers, destination, node_ids, cell_ids, cell_centers):
    vmem = pl.BlockSpec(memory_space=pltpu.VMEM)
    dma = pltpu.SemaphoreType.DMA
    inputs = (midpoints, line_vectors, burgers, destination.reshape(1, SEG), node_ids, cell_ids.reshape(1, SEG), cell_centers)
    inputs = [pltpu.with_memory_space_constraint(value, pltpu.HBM) for value in inputs]
    return pl.pallas_call(
        kernel,
        out_shape=(jax.ShapeDtypeStruct((3, 2 * SEG), F32), jax.ShapeDtypeStruct((3, 256), F32)),
        in_specs=[pl.BlockSpec(memory_space=pltpu.HBM)] * 7,
        out_specs=(vmem, vmem),
        scratch_shapes=[
            pltpu.VMEM((3, SEG), F32),
            pltpu.VMEM((3, SEG), F32),
            pltpu.VMEM((3, SEG), F32),
            pltpu.VMEM((1, SEG), I32),
            pltpu.VMEM((2, SEG), I32),
            pltpu.VMEM((1, SEG), I32),
            pltpu.VMEM((3, REGIONS * LANES), F32),
            dma((7,)),
            pltpu.VMEM((4 * (REGIONS - 1), LANES, TILE), BF16),
            pltpu.VMEM((DOMAINS, 40, LANES), F32),
            pltpu.VMEM((4, SEG, LANES), F32),
            pltpu.VMEM((2, 2, 64, LANES), F32),
            pltpu.VMEM((40, LANES), F32),
            pltpu.VMEM((NY, 40, LANES), F32),
            pltpu.VMEM((NZ, 40, LANES), F32),
            pltpu.VMEM((REGIONS, 40, LANES), F32),
            pltpu.VMEM((DOMAINS * 8, LANES), F32),
            pltpu.VMEM((DOMAINS * 8, LANES), F32),
            pltpu.VMEM((LANES, 2 * SEG), BF16),
            pltpu.VMEM((DOMAINS, SEG), BF16),
            pltpu.VMEM((DOMAINS, SEG), F32),
            dma((DOMAINS,)), dma((DOMAINS,)), dma((NY,)), dma((NY,)), dma((NZ,)), dma((NZ,)),
            dma((REGIONS,)), dma((REGIONS,)), dma((DOMAINS,)), dma((DOMAINS,)),
        ],
        compiler_params=pltpu.CompilerParams(
            collective_id=0, has_side_effects=True, vmem_limit_bytes=32 << 20
        ),
    )(*inputs)


def solution(mesh):
    both = ("region", "domain")

    def program(*args):
        with jax.sharding.use_abstract_mesh(mesh.abstract_mesh):
            return jax.shard_map(
                body,
                mesh=mesh,
                in_specs=(P(None, both), P(None, both), P(None, both), P(both, None), P(None, both), P(both), P()),
                out_specs=(P(None, both), P(None, both)),
                check_vma=False,
            )(*args)

    return program
```

```python
import jax
import jax.numpy as jnp
from jax import lax
from jax.experimental import pallas as pl
from jax.experimental.pallas import tpu as pltpu
from jax.sharding import PartitionSpec as P

MESH = pl.DeviceIdType.MESH
F32, BF16, I32 = jnp.float32, jnp.bfloat16, jnp.int32
CORE2 = 0.01
REGIONS, DOMAINS, NZ, NY = 8, 32, 8, 4
SEG, TILE, CHUNK, LANES = 512, 256, 64, 128
CHUNKS = SEG // CHUNK


def split2(v):
    high = v.astype(BF16)
    return high, (v - high.astype(F32)).astype(BF16)


def split3(v):
    high = v.astype(BF16)
    rest = v - high.astype(F32)
    mid = rest.astype(BF16)
    return high, mid, (rest - mid.astype(F32)).astype(BF16)


def cross(b, l):
    return [b[1] * l[2] - b[2] * l[1], b[2] * l[0] - b[0] * l[2], b[0] * l[1] - b[1] * l[0]]


def rows_of(ref):
    return [ref[a : a + 1, :] for a in range(3)]


def mxu_sum(rows, steps):
    def run(*accs):
        for n, (left, right, turned) in enumerate(steps):
            unit, stage = n % 2, n // 2 % 2
            pltpu.matmul_push_rhs(right, stage, unit, transpose=turned)
            pltpu.matmul_acc_lhs(accs[unit], left, stage)
        total = pltpu.matmul_pop(accs[0])
        return total + pltpu.matmul_pop(accs[1]) if len(steps) > 1 else total

    return pl.run_scoped(run, *[pltpu.ACC(w)((rows, TILE), F32) for w in range(2)])


def padded(right):
    return jnp.concatenate([right, jnp.zeros((TILE - right.shape[0], right.shape[1]), right.dtype)], axis=0)


def dot_nt(left, right):
    tiles = [slice(k, k + TILE) for k in range(0, left.shape[1], TILE)]
    return mxu_sum(left.shape[0], [(left[:, k], padded(right[:, k]), True) for k in tiles])


def z_offset(i):
    odd = i % 2
    return odd * ((i + 1) // 2) + (1 - odd) * ((NZ - i // 2) % NZ)


def kernel(
    mid_in, lin_in, bur_in, dest_in, nid_in, cid_in, cen_in,
    slot_out, node_out,
    mid, lin, bur, dest, nid, cid, cen, in_sem, kern,
    geo, xb, wsc, mom, my_in, mz_in, mall, msg, arrived, nodehot, rankhot, desthot,
    geo_send, geo_recv, my_send, my_recv, mz_send, mz_recv, mr_send, mr_recv, out_send, out_recv,
):
    region, dom = lax.axis_index("region"), lax.axis_index("domain")
    z, y = dom // NY, dom % NY

    barrier = pltpu.get_barrier_semaphore()

    def greet_domain(k, c):
        pl.semaphore_signal(barrier, inc=1, device_id=(region, (dom + k) % DOMAINS), device_id_type=MESH)
        return c

    def greet_region(k, c):
        pl.semaphore_signal(barrier, inc=1, device_id=((region + k) % REGIONS, dom), device_id_type=MESH)
        return c

    lax.fori_loop(1, DOMAINS, greet_domain, 0)
    lax.fori_loop(1, REGIONS, greet_region, 0)

    pairs_in = zip((mid_in, lin_in, bur_in, dest_in, nid_in, cid_in, cen_in), (mid, lin, bur, dest, nid, cid, cen))
    loads = [pltpu.make_async_copy(there, here, in_sem.at[n]) for n, (there, here) in enumerate(pairs_in)]
    for load in loads:
        load.start()

    def empty(*accs):
        for acc in accs:
            pltpu.matmul_pop(acc)

    pl.run_scoped(empty, *[pltpu.ACC(w)((SEG, TILE), F32) for w in range(2)])

    for load in loads:
        load.wait()

    middle = [(region.astype(F32) + 0.5) / REGIONS, 0.5, 0.5]
    m = [mid[a : a + 1, :] - middle[a] for a in range(3)]
    l, b = rows_of(lin), rows_of(bur)
    for c, row in enumerate(m + l + b):
        for j in range(4):
            geo[0, 4 * c + j : 4 * c + j + 1, :] = row[:, j * LANES : (j + 1) * LANES]
    for j in range(4):
        geo[0, 36 + j : 37 + j, :] = jnp.zeros((1, LANES), F32)

    outer = [b[i] * l[j] for i in range(3) for j in range(3)]
    q = cross(b, l)
    zero = jnp.zeros((1, SEG), F32)
    feats = outer + [outer[k] * m[a] for a in range(3) for k in range(9)]
    feats = jnp.concatenate(feats + q + [zero], axis=0)
    cell_hot = (lax.broadcasted_iota(I32, (LANES, SEG), 0) == cid[...]).astype(F32).astype(BF16)
    feats = [jnp.concatenate([part, jnp.zeros((8, SEG), BF16)], axis=0) for part in split3(feats)]
    parts = dot_nt(jnp.concatenate(feats, axis=0), cell_hot)[:, 0:LANES]
    mom[...] = parts[0:40] + parts[48:88] + parts[96:136]

    def y_copy(k):
        return pltpu.make_async_remote_copy(
            src_ref=mom, dst_ref=my_in.at[k], send_sem=my_send.at[k], recv_sem=my_recv.at[k],
            device_id=(region, z * NY + (y + k) % NY), device_id_type=MESH)

    def geo_copy(source, k, peer):
        return pltpu.make_async_remote_copy(
            src_ref=geo.at[source], dst_ref=geo.at[k], send_sem=geo_send.at[k], recv_sem=geo_recv.at[k],
            device_id=(region, peer), device_id_type=MESH)

    def geo_along_z(i):
        return geo_copy(0, i, ((z + z_offset(i)) % NZ) * NY + y)

    def geo_along_y(source, step):
        return geo_copy(source, NZ + (NY - 1) * source + step - 1, z * NY + (y + step) % NY)

    def pass_on(source):
        for step in range(1, NY):
            geo_along_y(source, step).start()

    def z_copy(k):
        return pltpu.make_async_remote_copy(
            src_ref=mz_in.at[0], dst_ref=mz_in.at[k], send_sem=mz_send.at[k], recv_sem=mz_recv.at[k],
            device_id=(region, ((z + k) % NZ) * NY + y), device_id_type=MESH)

    def r_copy(k):
        return pltpu.make_async_remote_copy(
            src_ref=mall.at[0], dst_ref=mall.at[k], send_sem=mr_send.at[k], recv_sem=mr_recv.at[k],
            device_id=((region + k) % REGIONS, dom), device_id_type=MESH)

    def geo_wait(k):
        return geo_copy(0, k, z * NY + (y + 1) % NY)

    def start(copy):
        def run(k, c):
            copy(k).start()
            return c

        return run

    d = dest[...]
    hot = (lax.broadcasted_iota(I32, (DOMAINS, SEG), 0) == d).astype(F32)
    upper = lax.broadcasted_iota(I32, (TILE, TILE), 0) < lax.broadcasted_iota(I32, (TILE, TILE), 1)
    upper = upper.astype(F32).astype(BF16)
    first, second = hot[:, 0:TILE].astype(BF16), hot[:, TILE:SEG].astype(BF16)
    ones = jnp.ones((TILE, TILE), BF16)
    before = jnp.concatenate(
        [mxu_sum(DOMAINS, [(first, upper, False)]), mxu_sum(DOMAINS, [(second, upper, False), (first, ones, False)])], axis=1
    )
    rank = jnp.sum(before * hot, axis=0, keepdims=True)
    desthot[...] = hot
    rankhot[...] = (lax.broadcasted_iota(I32, (DOMAINS, SEG), 0).astype(F32) == rank).astype(F32).astype(BF16)
    for e in range(2):
        low = nid[e : e + 1, :] & (LANES - 1)
        nodehot[:, e * SEG : (e + 1) * SEG] = (lax.broadcasted_iota(I32, (LANES, SEG), 0) == low).astype(F32).astype(BF16)

    own = jnp.concatenate([-2.0 * m[a] for a in range(3)] + [m[0] * m[0] + m[1] * m[1] + m[2] * m[2] + CORE2] + [zero] * 4, axis=0)
    columns = jnp.transpose(own)
    for a in range(4):
        xb[a] = jnp.broadcast_to(columns[:, a : a + 1], (SEG, LANES))
    wsc[...] = jnp.zeros_like(wsc)

    at = pl.ds(pl.multiple_of(region * LANES, LANES), LANES)
    target = jnp.transpose(jnp.concatenate([cen[0:3, at], jnp.zeros((5, LANES), F32)], axis=0))
    target = [jnp.broadcast_to(target[:, a : a + 1], (LANES, LANES)) for a in range(3)]
    for k in range(1, REGIONS):
        source = pl.ds(pl.multiple_of(((region + REGIONS - k) % REGIONS) * LANES, LANES), LANES)
        diff = [target[a] - cen[a : a + 1, source] for a in range(3)]
        g1 = lax.rsqrt(diff[0] * diff[0] + diff[1] * diff[1] + diff[2] * diff[2] + CORE2)
        g3 = g1 * g1 * g1
        for p, part in enumerate([g1] + [diff[a] * g3 for a in range(3)]):
            kern[4 * (k - 1) + p] = jnp.concatenate(split2(part), axis=1)

    def pairs(*accs):
        acc1, acc3 = accs[:CHUNKS], accs[CHUNKS:]
        blank = jnp.zeros((TILE - 32, TILE), BF16)

        def prepare(k, slot):
            v = [geo[k, 4 * c : 4 * c + 4, :] for c in range(9)]
            vm, vl, vb = v[0:3], v[3:6], v[6:9]
            vq = cross(vb, vl)
            for i in range(3):
                for j in range(3):
                    at = 4 * (3 * i + j)
                    wsc[slot, 0, at : at + 4, :] = vb[i] * vl[j]
                    wsc[slot, 1, at : at + 4, :] = vq[i] * vm[j]
                wsc[slot, 1, 36 + 4 * i : 40 + 4 * i, :] = vq[i]

        def push(slot, t):
            for w in range(2):
                wide = jnp.concatenate([wsc[slot, w, pl.ds(2 * t + u, 16, stride=4), :] for u in range(2)], axis=1)
                high, low = split2(wide)
                pltpu.matmul_push_rhs(jnp.concatenate([high, low, blank], axis=0), t, w, transpose=True)

        def stream(k, t):
            s = [
                jnp.concatenate([geo[k, 4 * a + 2 * t + u : 4 * a + 2 * t + u + 1, :] for u in range(2)], axis=1)
                for a in range(3)
            ]
            s2 = s[0] * s[0] + s[1] * s[1] + s[2] * s[2]
            for c in range(CHUNKS):
                x = [jnp.concatenate([xb[a, c * CHUNK : (c + 1) * CHUNK, :]] * 2, axis=1) for a in range(4)]
                g1 = lax.rsqrt((x[3] + s2) + x[0] * s[0] + x[1] * s[1] + x[2] * s[2])
                h1, l1 = split2(g1)
                h3, l3 = split2(g1 * g1 * g1)
                first = t if c == 0 else None
                pltpu.matmul_acc_lhs(acc1[c], h1, first)
                pltpu.matmul_acc_lhs(acc3[c], h3, first)
                pltpu.matmul_acc_lhs(acc1[c], l1)
                pltpu.matmul_acc_lhs(acc3[c], l3)

        def block(k, carry, passing=False):
            push(k % 2, 1)
            stream(k, 0)
            geo_wait(k + 1).wait_recv()
            if passing:
                pass_on(k + 1)
            prepare(k + 1, (k + 1) % 2)
            push((k + 1) % 2, 0)
            stream(k, 1)
            return carry

        prepare(0, 0)
        push(0, 0)
        push(0, 1)
        stream(0, 0)
        stream(0, 1)

        pl.semaphore_wait(barrier, DOMAINS - 1 + REGIONS - 1)
        for k in range(1, NY):
            y_copy(k).start()
        lax.fori_loop(1, NZ, start(geo_along_z), 0)
        pass_on(0)
        geo_wait(1).wait_recv()
        pass_on(1)
        prepare(1, 1)
        push(1, 0)
        lax.fori_loop(1, NZ - 1, lambda k, c: block(k, c, True), 0)
        for k in range(1, NY):
            y_copy(k).wait_recv()
        mz_in[0] = mom[...] + my_in[1] + my_in[2] + my_in[3]
        for k in range(1, NZ):
            z_copy(k).start()
        lax.fori_loop(NZ - 1, 16, block, 0)
        for k in range(1, NZ):
            z_copy(k).wait_recv()
        total = mz_in[0]
        for k in range(1, NZ):
            total = total + mz_in[k]
        center = [cen[a : a + 1, pl.ds(pl.multiple_of(region * LANES, LANES), LANES)] - middle[a] for a in range(3)]
        mall[0, 0:9, :] = total[0:9]
        for a in range(3):
            for k in range(9):
                at = 9 + 9 * a + k
                value = total[at : at + 1] - center[a] * total[k : k + 1]
                if k % 3 == a:
                    value = value + total[36 + k // 3 : 37 + k // 3]
                mall[0, at : at + 1, :] = value
        mall[0, 36:40, :] = jnp.zeros((4, LANES), F32)
        for k in range(1, REGIONS):
            r_copy(k).start()
        lax.fori_loop(16, DOMAINS - 1, block, 0)
        push((DOMAINS - 1) % 2, 1)
        stream(DOMAINS - 1, 0)
        stream(DOMAINS - 1, 1)
        for c in range(CHUNKS):
            one, three = pltpu.matmul_pop(acc1[c]), pltpu.matmul_pop(acc3[c])
            xb[0, c * CHUNK : (c + 1) * CHUNK, :] = one[:, 0:LANES]
            xb[1, c * CHUNK : (c + 1) * CHUNK, :] = three[:, 0:LANES]

    pl.run_scoped(pairs, *[pltpu.ACC(w)((CHUNK, TILE), F32) for w in range(2) for _ in range(CHUNKS)])

    for k in range(1, REGIONS):
        r_copy(k).wait_recv()
    steps = []
    for k in range(1, REGIONS):
        total = mall[k]
        for p in range(4):
            wh, wl = split2(jnp.concatenate([total[9 * p : 9 * p + 9], jnp.zeros((7, LANES), F32)], axis=0))
            both = jnp.concatenate([wh, wl], axis=0)
            steps.append((jnp.concatenate([both, both], axis=1), padded(kern[4 * (k - 1) + p]), True))
    far = mxu_sum(32, steps)
    far = split3(far[0:16, 0:LANES] + far[16:32, 0:LANES])
    cell_hot = (lax.broadcasted_iota(I32, (TILE, SEG), 0) % LANES == cid[...]).astype(F32).astype(BF16)
    pair = [jnp.concatenate(far[0:2], axis=1), jnp.concatenate([far[2], jnp.zeros_like(far[2])], axis=1)]
    far = jnp.concatenate(
        [mxu_sum(16, [(left, cell_hot[:, k : k + TILE], False) for left in pair]) for k in (0, TILE)], axis=1
    )

    one, three = jnp.transpose(xb[0]), jnp.transpose(xb[1])
    one = one[0:16] + one[16:32]
    three = three[0:16] + three[16:32]
    x = [mid[a : a + 1, :] - middle[a] for a in range(3)]
    b = rows_of(bur)
    stress = [
        one[k : k + 1] + far[k : k + 1] + three[9 + k // 3 : 10 + k // 3] * x[k % 3] - three[k : k + 1] for k in range(9)
    ]
    force = []
    for i in range(3):
        total = zero
        for j in range(3):
            total = total + 0.5 * (stress[3 * i + j] + stress[3 * j + i]) * b[j]
        force.append(total)

    halves = [0.5 * f for f in force]
    table = jnp.concatenate([halves[0]] * 2 + [halves[1]] * 2 + [halves[2]] * 2 + [zero] * 2, axis=0)
    table_high = table.astype(BF16).astype(F32)
    table_low = table - table_high
    sub = lax.broadcasted_iota(I32, (8, SEG), 0) % 2
    lefts = []
    for e in range(2):
        row = (nid[e : e + 1, :] // LANES) - sub
        hits = [row == 2 * owner for owner in range(DOMAINS)]
        for part in (table_high, table_low):
            lefts.append(jnp.concatenate([jnp.where(hit, part, 0.0) for hit in hits], axis=0).astype(BF16))
    rights = [nodehot[:, e * SEG : (e + 1) * SEG] for e in (0, 0, 1, 1)]
    nodes = dot_nt(jnp.concatenate(lefts, axis=1), jnp.concatenate(rights, axis=1))
    hot = desthot[...]
    left = [part for c in range(3) for part in split3(hot * force[c])]
    part = dot_nt(jnp.concatenate(left, axis=0), rankhot[...])[:, 0:32]
    slots = [part[96 * c : 96 * c + 32] + part[96 * c + 32 : 96 * c + 64] + part[96 * c + 64 : 96 * c + 96] for c in range(3)]
    slots = jnp.concatenate(slots + [jnp.zeros((DOMAINS, 32), F32)], axis=1)
    msg[...] = nodes[:, 0:LANES]
    msg[pl.ds(6, DOMAINS, stride=8), :] = slots

    def out_copy(k):
        peer = (dom + k) % DOMAINS
        return pltpu.make_async_remote_copy(
            src_ref=msg.at[pl.ds(pl.multiple_of(8 * peer, 8), 8), :],
            dst_ref=arrived.at[pl.ds(pl.multiple_of(8 * dom, 8), 8), :],
            send_sem=out_send.at[k], recv_sem=out_recv.at[k],
            device_id=(region, peer), device_id_type=MESH)

    lax.fori_loop(1, DOMAINS, start(out_copy), 0)
    mine = pl.ds(pl.multiple_of(8 * dom, 8), 8)
    arrived[mine, :] = msg[mine, :]

    def received(k, c):
        out_copy(k).wait_recv()
        return c

    lax.fori_loop(1, DOMAINS, received, 0)
    total = arrived[0:8, :]
    for s in range(1, DOMAINS):
        total = total + arrived[8 * s : 8 * s + 8, :]
    for c in range(3):
        for h in range(2):
            node_out[c : c + 1, h * LANES : (h + 1) * LANES] = total[2 * c + h : 2 * c + h + 1]
    quarter = lax.broadcasted_iota(I32, (8, LANES), 1) // 32
    four = [arrived[pl.ds(6 + 8 * a, 8, stride=32), :] for a in range(4)]
    for c in range(3):
        line = jnp.zeros((8, LANES), F32)
        for a in range(4):
            turn = (32 * (a - c)) % LANES
            line = jnp.where(quarter == a, pltpu.roll(four[a], turn, 1) if turn else four[a], line)
        for j in range(8):
            slot_out[c : c + 1, j * LANES : (j + 1) * LANES] = line[j : j + 1]

    for copy, count in ((y_copy, NY), (geo_wait, DOMAINS), (z_copy, NZ), (r_copy, REGIONS), (out_copy, DOMAINS)):

        def sent(k, c, copy=copy):
            copy(k).wait_send()
            return c

        lax.fori_loop(1, count, sent, 0)


def body(midpoints, line_vectors, burgers, destination, node_ids, cell_ids, cell_centers):
    vmem = pl.BlockSpec(memory_space=pltpu.VMEM)
    dma = pltpu.SemaphoreType.DMA
    inputs = (midpoints, line_vectors, burgers, destination.reshape(1, SEG), node_ids, cell_ids.reshape(1, SEG), cell_centers)
    inputs = [pltpu.with_memory_space_constraint(value, pltpu.HBM) for value in inputs]
    return pl.pallas_call(
        kernel,
        out_shape=(jax.ShapeDtypeStruct((3, 2 * SEG), F32), jax.ShapeDtypeStruct((3, 256), F32)),
        in_specs=[pl.BlockSpec(memory_space=pltpu.HBM)] * 7,
        out_specs=(vmem, vmem),
        scratch_shapes=[
            pltpu.VMEM((3, SEG), F32),
            pltpu.VMEM((3, SEG), F32),
            pltpu.VMEM((3, SEG), F32),
            pltpu.VMEM((1, SEG), I32),
            pltpu.VMEM((2, SEG), I32),
            pltpu.VMEM((1, SEG), I32),
            pltpu.VMEM((3, REGIONS * LANES), F32),
            dma((7,)),
            pltpu.VMEM((4 * (REGIONS - 1), LANES, TILE), BF16),
            pltpu.VMEM((DOMAINS, 40, LANES), F32),
            pltpu.VMEM((4, SEG, LANES), F32),
            pltpu.VMEM((2, 2, 64, LANES), F32),
            pltpu.VMEM((40, LANES), F32),
            pltpu.VMEM((NY, 40, LANES), F32),
            pltpu.VMEM((NZ, 40, LANES), F32),
            pltpu.VMEM((REGIONS, 40, LANES), F32),
            pltpu.VMEM((DOMAINS * 8, LANES), F32),
            pltpu.VMEM((DOMAINS * 8, LANES), F32),
            pltpu.VMEM((LANES, 2 * SEG), BF16),
            pltpu.VMEM((DOMAINS, SEG), BF16),
            pltpu.VMEM((DOMAINS, SEG), F32),
            dma((DOMAINS,)), dma((DOMAINS,)), dma((NY,)), dma((NY,)), dma((NZ,)), dma((NZ,)),
            dma((REGIONS,)), dma((REGIONS,)), dma((DOMAINS,)), dma((DOMAINS,)),
        ],
        compiler_params=pltpu.CompilerParams(
            collective_id=0, has_side_effects=True, vmem_limit_bytes=32 << 20
        ),
    )(*inputs)


def solution(mesh):
    both = ("region", "domain")

    def program(*args):
        with jax.sharding.use_abstract_mesh(mesh.abstract_mesh):
            return jax.shard_map(
                body,
                mesh=mesh,
                in_specs=(P(None, both), P(None, both), P(None, both), P(both, None), P(None, both), P(both), P()),
                out_specs=(P(None, both), P(None, both)),
                check_vma=False,
            )(*args)

    return program
```

```python
import jax
import jax.numpy as jnp
from jax import lax
from jax.experimental import pallas as pl
from jax.experimental.pallas import tpu as pltpu
from jax.sharding import PartitionSpec as P

MESH = pl.DeviceIdType.MESH
F32, BF16, I32 = jnp.float32, jnp.bfloat16, jnp.int32
CORE2 = 0.01
REGIONS, DOMAINS, NZ, NY = 8, 32, 8, 4
SEG, TILE, CHUNK, LANES = 512, 256, 64, 128
CHUNKS = SEG // CHUNK


def split2(v):
    high = v.astype(BF16)
    return high, (v - high.astype(F32)).astype(BF16)


def split3(v):
    high = v.astype(BF16)
    rest = v - high.astype(F32)
    mid = rest.astype(BF16)
    return high, mid, (rest - mid.astype(F32)).astype(BF16)


def cross(b, l):
    return [b[1] * l[2] - b[2] * l[1], b[2] * l[0] - b[0] * l[2], b[0] * l[1] - b[1] * l[0]]


def rows_of(ref):
    return [ref[a : a + 1, :] for a in range(3)]


def mxu_sum(rows, steps):
    def run(*accs):
        for n, (left, right, turned) in enumerate(steps):
            unit, stage = n % 2, n // 2 % 2
            pltpu.matmul_push_rhs(right, stage, unit, transpose=turned)
            pltpu.matmul_acc_lhs(accs[unit], left, stage)
        total = pltpu.matmul_pop(accs[0])
        return total + pltpu.matmul_pop(accs[1]) if len(steps) > 1 else total

    return pl.run_scoped(run, *[pltpu.ACC(w)((rows, TILE), F32) for w in range(2)])


def padded(right):
    return jnp.concatenate([right, jnp.zeros((TILE - right.shape[0], right.shape[1]), right.dtype)], axis=0)


def dot_nt(left, right):
    tiles = [slice(k, k + TILE) for k in range(0, left.shape[1], TILE)]
    return mxu_sum(left.shape[0], [(left[:, k], padded(right[:, k]), True) for k in tiles])


def z_offset(i):
    odd = i % 2
    return odd * ((i + 1) // 2) + (1 - odd) * ((NZ - i // 2) % NZ)


def kernel(
    mid_in, lin_in, bur_in, dest_in, nid_in, cid_in, cen_in,
    slot_out, node_out,
    mid, lin, bur, dest, nid, cid, cen, in_sem, kern,
    geo, xb, wsc, mom, my_in, mz_in, mall, msg, arrived, nodehot, rankhot, desthot,
    geo_send, geo_recv, my_send, my_recv, mz_send, mz_recv, mr_send, mr_recv, out_send, out_recv,
):
    region, dom = lax.axis_index("region"), lax.axis_index("domain")
    z, y = dom // NY, dom % NY

    barrier = pltpu.get_barrier_semaphore()

    def greet_domain(k, c):
        pl.semaphore_signal(barrier, inc=1, device_id=(region, (dom + k) % DOMAINS), device_id_type=MESH)
        return c

    def greet_region(k, c):
        pl.semaphore_signal(barrier, inc=1, device_id=((region + k) % REGIONS, dom), device_id_type=MESH)
        return c

    lax.fori_loop(1, DOMAINS, greet_domain, 0)
    lax.fori_loop(1, REGIONS, greet_region, 0)

    pairs_in = zip((mid_in, lin_in, bur_in, dest_in, nid_in, cid_in, cen_in), (mid, lin, bur, dest, nid, cid, cen))
    loads = [pltpu.make_async_copy(there, here, in_sem.at[n]) for n, (there, here) in enumerate(pairs_in)]
    for load in loads:
        load.start()

    def empty(*accs):
        for acc in accs:
            pltpu.matmul_pop(acc)

    pl.run_scoped(empty, *[pltpu.ACC(w)((SEG, TILE), F32) for w in range(2)])

    for load in loads:
        load.wait()

    middle = [(region.astype(F32) + 0.5) / REGIONS, 0.5, 0.5]
    m = [mid[a : a + 1, :] - middle[a] for a in range(3)]
    l, b = rows_of(lin), rows_of(bur)
    for c, row in enumerate(m + l + b):
        for j in range(4):
            geo[0, 4 * c + j : 4 * c + j + 1, :] = row[:, j * LANES : (j + 1) * LANES]
    for j in range(4):
        geo[0, 36 + j : 37 + j, :] = jnp.zeros((1, LANES), F32)

    outer = [b[i] * l[j] for i in range(3) for j in range(3)]
    q = cross(b, l)
    zero = jnp.zeros((1, SEG), F32)
    feats = outer + [outer[k] * m[a] for a in range(3) for k in range(9)]
    feats = jnp.concatenate(feats + q + [zero], axis=0)
    cell_hot = (lax.broadcasted_iota(I32, (LANES, SEG), 0) == cid[...]).astype(F32).astype(BF16)
    feats = [jnp.concatenate([part, jnp.zeros((8, SEG), BF16)], axis=0) for part in split3(feats)]
    parts = dot_nt(jnp.concatenate(feats, axis=0), cell_hot)[:, 0:LANES]
    mom[...] = parts[0:40] + parts[48:88] + parts[96:136]

    def y_copy(k):
        return pltpu.make_async_remote_copy(
            src_ref=mom, dst_ref=my_in.at[k], send_sem=my_send.at[k], recv_sem=my_recv.at[k],
            device_id=(region, z * NY + (y + k) % NY), device_id_type=MESH)

    def geo_copy(source, k, peer):
        return pltpu.make_async_remote_copy(
            src_ref=geo.at[source], dst_ref=geo.at[k], send_sem=geo_send.at[k], recv_sem=geo_recv.at[k],
            device_id=(region, peer), device_id_type=MESH)

    def geo_along_z(i):
        return geo_copy(0, i, ((z + z_offset(i)) % NZ) * NY + y)

    def geo_along_y(source, step):
        return geo_copy(source, NZ + (NY - 1) * source + step - 1, z * NY + (y + step) % NY)

    def pass_on(source):
        for step in range(1, NY):
            geo_along_y(source, step).start()

    def z_copy(k):
        return pltpu.make_async_remote_copy(
            src_ref=mz_in.at[0], dst_ref=mz_in.at[k], send_sem=mz_send.at[k], recv_sem=mz_recv.at[k],
            device_id=(region, ((z + k) % NZ) * NY + y), device_id_type=MESH)

    def r_copy(k):
        return pltpu.make_async_remote_copy(
            src_ref=mall.at[0], dst_ref=mall.at[k], send_sem=mr_send.at[k], recv_sem=mr_recv.at[k],
            device_id=((region + k) % REGIONS, dom), device_id_type=MESH)

    def geo_wait(k):
        return geo_copy(0, k, z * NY + (y + 1) % NY)

    def start(copy):
        def run(k, c):
            copy(k).start()
            return c

        return run

    d = dest[...]
    hot = (lax.broadcasted_iota(I32, (DOMAINS, SEG), 0) == d).astype(F32)
    upper = lax.broadcasted_iota(I32, (TILE, TILE), 0) < lax.broadcasted_iota(I32, (TILE, TILE), 1)
    upper = upper.astype(F32).astype(BF16)
    first, second = hot[:, 0:TILE].astype(BF16), hot[:, TILE:SEG].astype(BF16)
    ones = jnp.ones((TILE, TILE), BF16)
    before = jnp.concatenate(
        [mxu_sum(DOMAINS, [(first, upper, False)]), mxu_sum(DOMAINS, [(second, upper, False), (first, ones, False)])], axis=1
    )
    rank = jnp.sum(before * hot, axis=0, keepdims=True)
    desthot[...] = hot
    rankhot[...] = (lax.broadcasted_iota(I32, (DOMAINS, SEG), 0).astype(F32) == rank).astype(F32).astype(BF16)
    for e in range(2):
        low = nid[e : e + 1, :] & (LANES - 1)
        nodehot[:, e * SEG : (e + 1) * SEG] = (lax.broadcasted_iota(I32, (LANES, SEG), 0) == low).astype(F32).astype(BF16)

    own = jnp.concatenate([-2.0 * m[a] for a in range(3)] + [m[0] * m[0] + m[1] * m[1] + m[2] * m[2] + CORE2] + [zero] * 4, axis=0)
    columns = jnp.transpose(own)
    for a in range(4):
        xb[a] = jnp.broadcast_to(columns[:, a : a + 1], (SEG, LANES))
    wsc[...] = jnp.zeros_like(wsc)

    at = pl.ds(pl.multiple_of(region * LANES, LANES), LANES)
    target = jnp.transpose(jnp.concatenate([cen[0:3, at], jnp.zeros((5, LANES), F32)], axis=0))
    target = [jnp.broadcast_to(target[:, a : a + 1], (LANES, LANES)) for a in range(3)]
    for k in range(1, REGIONS):
        source = pl.ds(pl.multiple_of(((region + REGIONS - k) % REGIONS) * LANES, LANES), LANES)
        diff = [target[a] - cen[a : a + 1, source] for a in range(3)]
        g1 = lax.rsqrt(diff[0] * diff[0] + diff[1] * diff[1] + diff[2] * diff[2] + CORE2)
        g3 = g1 * g1 * g1
        for p, part in enumerate([g1] + [diff[a] * g3 for a in range(3)]):
            kern[4 * (k - 1) + p] = jnp.concatenate(split2(part), axis=1)

    def pairs(*accs):
        acc1, acc3 = accs[:CHUNKS], accs[CHUNKS:]
        blank = jnp.zeros((TILE - 32, TILE), BF16)

        def prepare(k, slot):
            v = [geo[k, 4 * c : 4 * c + 4, :] for c in range(9)]
            vm, vl, vb = v[0:3], v[3:6], v[6:9]
            vq = cross(vb, vl)
            for i in range(3):
                for j in range(3):
                    at = 4 * (3 * i + j)
                    wsc[slot, 0, at : at + 4, :] = vb[i] * vl[j]
                    wsc[slot, 1, at : at + 4, :] = vq[i] * vm[j]
                wsc[slot, 1, 36 + 4 * i : 40 + 4 * i, :] = vq[i]

        def push(slot, t):
            for w in range(2):
                wide = jnp.concatenate([wsc[slot, w, pl.ds(2 * t + u, 16, stride=4), :] for u in range(2)], axis=1)
                high, low = split2(wide)
                pltpu.matmul_push_rhs(jnp.concatenate([high, low, blank], axis=0), t, w, transpose=True)

        def stream(k, t):
            s = [
                jnp.concatenate([geo[k, 4 * a + 2 * t + u : 4 * a + 2 * t + u + 1, :] for u in range(2)], axis=1)
                for a in range(3)
            ]
            s2 = s[0] * s[0] + s[1] * s[1] + s[2] * s[2]
            for c in range(CHUNKS):
                x = [jnp.concatenate([xb[a, c * CHUNK : (c + 1) * CHUNK, :]] * 2, axis=1) for a in range(4)]
                g1 = lax.rsqrt((x[3] + s2) + x[0] * s[0] + x[1] * s[1] + x[2] * s[2])
                h1, l1 = split2(g1)
                h3, l3 = split2(g1 * g1 * g1)
                first = t if c == 0 else None
                pltpu.matmul_acc_lhs(acc1[c], h1, first)
                pltpu.matmul_acc_lhs(acc3[c], h3, first)
                pltpu.matmul_acc_lhs(acc1[c], l1)
                pltpu.matmul_acc_lhs(acc3[c], l3)

        def column_moments():
            for k in range(1, NY):
                y_copy(k).wait_recv()
            mz_in[0] = mom[...] + my_in[1] + my_in[2] + my_in[3]
            for k in range(1, NZ):
                z_copy(k).start()

        def region_moments():
            for k in range(1, NZ):
                z_copy(k).wait_recv()
            total = mz_in[0]
            for k in range(1, NZ):
                total = total + mz_in[k]
            center = [cen[a : a + 1, pl.ds(pl.multiple_of(region * LANES, LANES), LANES)] - middle[a] for a in range(3)]
            mall[0, 0:9, :] = total[0:9]
            for a in range(3):
                for k in range(9):
                    at = 9 + 9 * a + k
                    value = total[at : at + 1] - center[a] * total[k : k + 1]
                    if k % 3 == a:
                        value = value + total[36 + k // 3 : 37 + k // 3]
                    mall[0, at : at + 1, :] = value
            mall[0, 36:40, :] = jnp.zeros((4, LANES), F32)
            for k in range(1, REGIONS):
                r_copy(k).start()

        def block(k, carry):
            push(k % 2, 1)
            stream(k, 0)
            later = (k + 1) - (k + 1) // DOMAINS

            @pl.when(k < DOMAINS - 1)
            def _():
                geo_wait(later).wait_recv()

            @pl.when(k < NZ - 1)
            def _():
                pass_on(later)

            @pl.when(k == NZ - 2)
            def _():
                column_moments()

            @pl.when(k == 15)
            def _():
                region_moments()

            prepare(later, (k + 1) % 2)
            push((k + 1) % 2, 0)
            stream(k, 1)
            return carry

        prepare(0, 0)
        push(0, 0)
        push(0, 1)
        stream(0, 0)
        stream(0, 1)

        pl.semaphore_wait(barrier, DOMAINS - 1 + REGIONS - 1)
        lax.fori_loop(1, NZ, start(geo_along_z), 0)
        for k in range(1, NY):
            y_copy(k).start()
        pass_on(0)
        geo_wait(1).wait_recv()
        pass_on(1)
        prepare(1, 1)
        push(1, 0)
        lax.fori_loop(1, DOMAINS, block, 0)
        pltpu.matmul_acc_lhs(acc1[0], jnp.zeros((CHUNK, TILE), BF16), 0)
        pltpu.matmul_acc_lhs(acc3[0], jnp.zeros((CHUNK, TILE), BF16), 0)
        for c in range(CHUNKS):
            one, three = pltpu.matmul_pop(acc1[c]), pltpu.matmul_pop(acc3[c])
            xb[0, c * CHUNK : (c + 1) * CHUNK, :] = one[:, 0:LANES]
            xb[1, c * CHUNK : (c + 1) * CHUNK, :] = three[:, 0:LANES]

    pl.run_scoped(pairs, *[pltpu.ACC(w)((CHUNK, TILE), F32) for w in range(2) for _ in range(CHUNKS)])

    for k in range(1, REGIONS):
        r_copy(k).wait_recv()
    steps = []
    for k in range(1, REGIONS):
        total = mall[k]
        for p in range(4):
            wh, wl = split2(jnp.concatenate([total[9 * p : 9 * p + 9], jnp.zeros((7, LANES), F32)], axis=0))
            both = jnp.concatenate([wh, wl], axis=0)
            steps.append((jnp.concatenate([both, both], axis=1), padded(kern[4 * (k - 1) + p]), True))
    far = mxu_sum(32, steps)
    far = split3(far[0:16, 0:LANES] + far[16:32, 0:LANES])
    cell_hot = (lax.broadcasted_iota(I32, (TILE, SEG), 0) % LANES == cid[...]).astype(F32).astype(BF16)
    pair = [jnp.concatenate(far[0:2], axis=1), jnp.concatenate([far[2], jnp.zeros_like(far[2])], axis=1)]
    far = jnp.concatenate(
        [mxu_sum(16, [(left, cell_hot[:, k : k + TILE], False) for left in pair]) for k in (0, TILE)], axis=1
    )

    one, three = jnp.transpose(xb[0]), jnp.transpose(xb[1])
    one = one[0:16] + one[16:32]
    three = three[0:16] + three[16:32]
    x = [mid[a : a + 1, :] - middle[a] for a in range(3)]
    b = rows_of(bur)
    stress = [
        one[k : k + 1] + far[k : k + 1] + three[9 + k // 3 : 10 + k // 3] * x[k % 3] - three[k : k + 1] for k in range(9)
    ]
    force = []
    for i in range(3):
        total = zero
        for j in range(3):
            total = total + 0.5 * (stress[3 * i + j] + stress[3 * j + i]) * b[j]
        force.append(total)

    halves = [0.5 * f for f in force]
    table = jnp.concatenate([halves[0]] * 2 + [halves[1]] * 2 + [halves[2]] * 2 + [zero] * 2, axis=0)
    table_high = table.astype(BF16).astype(F32)
    table_low = table - table_high
    sub = lax.broadcasted_iota(I32, (8, SEG), 0) % 2
    lefts = []
    for e in range(2):
        row = (nid[e : e + 1, :] // LANES) - sub
        hits = [row == 2 * owner for owner in range(DOMAINS)]
        for part in (table_high, table_low):
            lefts.append(jnp.concatenate([jnp.where(hit, part, 0.0) for hit in hits], axis=0).astype(BF16))
    rights = [nodehot[:, e * SEG : (e + 1) * SEG] for e in (0, 0, 1, 1)]
    nodes = dot_nt(jnp.concatenate(lefts, axis=1), jnp.concatenate(rights, axis=1))
    hot = desthot[...]
    left = [part for c in range(3) for part in split3(hot * force[c])]
    part = dot_nt(jnp.concatenate(left, axis=0), rankhot[...])[:, 0:32]
    slots = [part[96 * c : 96 * c + 32] + part[96 * c + 32 : 96 * c + 64] + part[96 * c + 64 : 96 * c + 96] for c in range(3)]
    slots = jnp.concatenate(slots + [jnp.zeros((DOMAINS, 32), F32)], axis=1)
    msg[...] = nodes[:, 0:LANES]
    msg[pl.ds(6, DOMAINS, stride=8), :] = slots

    def out_copy(k):
        peer = (dom + DOMAINS // 2 + (k % 2) * (k // 2) + (1 - k % 2) * (DOMAINS - k // 2)) % DOMAINS
        return pltpu.make_async_remote_copy(
            src_ref=msg.at[pl.ds(pl.multiple_of(8 * peer, 8), 8), :],
            dst_ref=arrived.at[pl.ds(pl.multiple_of(8 * dom, 8), 8), :],
            send_sem=out_send.at[k], recv_sem=out_recv.at[k],
            device_id=(region, peer), device_id_type=MESH)

    lax.fori_loop(1, DOMAINS, start(out_copy), 0)
    mine = pl.ds(pl.multiple_of(8 * dom, 8), 8)
    arrived[mine, :] = msg[mine, :]

    def received(k, c):
        out_copy(k).wait_recv()
        return c

    lax.fori_loop(1, DOMAINS, received, 0)
    total = arrived[0:8, :]
    for s in range(1, DOMAINS):
        total = total + arrived[8 * s : 8 * s + 8, :]
    for c in range(3):
        for h in range(2):
            node_out[c : c + 1, h * LANES : (h + 1) * LANES] = total[2 * c + h : 2 * c + h + 1]
    quarter = lax.broadcasted_iota(I32, (8, LANES), 1) // 32
    four = [arrived[pl.ds(6 + 8 * a, 8, stride=32), :] for a in range(4)]
    for c in range(3):
        line = jnp.zeros((8, LANES), F32)
        for a in range(4):
            turn = (32 * (a - c)) % LANES
            line = jnp.where(quarter == a, pltpu.roll(four[a], turn, 1) if turn else four[a], line)
        for j in range(8):
            slot_out[c : c + 1, j * LANES : (j + 1) * LANES] = line[j : j + 1]

    for copy, count in ((y_copy, NY), (geo_wait, DOMAINS), (z_copy, NZ), (r_copy, REGIONS), (out_copy, DOMAINS)):

        def sent(k, c, copy=copy):
            copy(k).wait_send()
            return c

        lax.fori_loop(1, count, sent, 0)


def body(midpoints, line_vectors, burgers, destination, node_ids, cell_ids, cell_centers):
    vmem = pl.BlockSpec(memory_space=pltpu.VMEM)
    dma = pltpu.SemaphoreType.DMA
    inputs = (midpoints, line_vectors, burgers, destination.reshape(1, SEG), node_ids, cell_ids.reshape(1, SEG), cell_centers)
    inputs = [pltpu.with_memory_space_constraint(value, pltpu.HBM) for value in inputs]
    return pl.pallas_call(
        kernel,
        out_shape=(jax.ShapeDtypeStruct((3, 2 * SEG), F32), jax.ShapeDtypeStruct((3, 256), F32)),
        in_specs=[pl.BlockSpec(memory_space=pltpu.HBM)] * 7,
        out_specs=(vmem, vmem),
        scratch_shapes=[
            pltpu.VMEM((3, SEG), F32),
            pltpu.VMEM((3, SEG), F32),
            pltpu.VMEM((3, SEG), F32),
            pltpu.VMEM((1, SEG), I32),
            pltpu.VMEM((2, SEG), I32),
            pltpu.VMEM((1, SEG), I32),
            pltpu.VMEM((3, REGIONS * LANES), F32),
            dma((7,)),
            pltpu.VMEM((4 * (REGIONS - 1), LANES, TILE), BF16),
            pltpu.VMEM((DOMAINS, 40, LANES), F32),
            pltpu.VMEM((4, SEG, LANES), F32),
            pltpu.VMEM((2, 2, 64, LANES), F32),
            pltpu.VMEM((40, LANES), F32),
            pltpu.VMEM((NY, 40, LANES), F32),
            pltpu.VMEM((NZ, 40, LANES), F32),
            pltpu.VMEM((REGIONS, 40, LANES), F32),
            pltpu.VMEM((DOMAINS * 8, LANES), F32),
            pltpu.VMEM((DOMAINS * 8, LANES), F32),
            pltpu.VMEM((LANES, 2 * SEG), BF16),
            pltpu.VMEM((DOMAINS, SEG), BF16),
            pltpu.VMEM((DOMAINS, SEG), F32),
            dma((DOMAINS,)), dma((DOMAINS,)), dma((NY,)), dma((NY,)), dma((NZ,)), dma((NZ,)),
            dma((REGIONS,)), dma((REGIONS,)), dma((DOMAINS,)), dma((DOMAINS,)),
        ],
        compiler_params=pltpu.CompilerParams(
            collective_id=0, has_side_effects=True, vmem_limit_bytes=32 << 20
        ),
    )(*inputs)


def solution(mesh):
    both = ("region", "domain")

    def program(*args):
        with jax.sharding.use_abstract_mesh(mesh.abstract_mesh):
            return jax.shard_map(
                body,
                mesh=mesh,
                in_specs=(P(None, both), P(None, both), P(None, both), P(both, None), P(None, both), P(both), P()),
                out_specs=(P(None, both), P(None, both)),
                check_vma=False,
            )(*args)

    return program
```

```python
import jax
import jax.numpy as jnp
from jax import lax
from jax.experimental import pallas as pl
from jax.experimental.pallas import tpu as pltpu
from jax.sharding import PartitionSpec as P

MESH = pl.DeviceIdType.MESH
F32, BF16, I32 = jnp.float32, jnp.bfloat16, jnp.int32
CORE2 = 0.01
REGIONS, DOMAINS, NZ, NY = 8, 32, 8, 4
SEG, TILE, CHUNK, LANES = 512, 256, 64, 128
CHUNKS = SEG // CHUNK


def split2(v):
    high = v.astype(BF16)
    return high, (v - high.astype(F32)).astype(BF16)


def split3(v):
    high = v.astype(BF16)
    rest = v - high.astype(F32)
    mid = rest.astype(BF16)
    return high, mid, (rest - mid.astype(F32)).astype(BF16)


def cross(b, l):
    return [b[1] * l[2] - b[2] * l[1], b[2] * l[0] - b[0] * l[2], b[0] * l[1] - b[1] * l[0]]


def rows_of(ref):
    return [ref[a : a + 1, :] for a in range(3)]


def mxu_sum(rows, steps):
    def run(*accs):
        for n, (left, right, turned) in enumerate(steps):
            unit, stage = n % 2, n // 2 % 2
            pltpu.matmul_push_rhs(right, stage, unit, transpose=turned)
            pltpu.matmul_acc_lhs(accs[unit], left, stage)
        total = pltpu.matmul_pop(accs[0])
        return total + pltpu.matmul_pop(accs[1]) if len(steps) > 1 else total

    return pl.run_scoped(run, *[pltpu.ACC(w)((rows, TILE), F32) for w in range(2)])


def padded(right):
    return jnp.concatenate([right, jnp.zeros((TILE - right.shape[0], right.shape[1]), right.dtype)], axis=0)


def dot_nt(left, right):
    tiles = [slice(k, k + TILE) for k in range(0, left.shape[1], TILE)]
    return mxu_sum(left.shape[0], [(left[:, k], padded(right[:, k]), True) for k in tiles])


def z_offset(i):
    odd = i % 2
    return odd * ((i + 1) // 2) + (1 - odd) * ((NZ - i // 2) % NZ)


def kernel(
    mid_in, lin_in, bur_in, dest_in, nid_in, cid_in, cen_in,
    slot_out, node_out,
    mid, lin, bur, dest, nid, cid, cen, in_sem, kern,
    geo, xb, wsc, mom, my_in, mz_in, mall, msg, arrived, nodehot, rankhot, desthot,
    geo_send, geo_recv, my_send, my_recv, mz_send, mz_recv, mr_send, mr_recv, out_send, out_recv,
):
    region, dom = lax.axis_index("region"), lax.axis_index("domain")
    z, y = dom // NY, dom % NY

    barrier = pltpu.get_barrier_semaphore()

    def greet_domain(k, c):
        pl.semaphore_signal(barrier, inc=1, device_id=(region, (dom + k) % DOMAINS), device_id_type=MESH)
        return c

    def greet_region(k, c):
        pl.semaphore_signal(barrier, inc=1, device_id=((region + k) % REGIONS, dom), device_id_type=MESH)
        return c

    lax.fori_loop(1, DOMAINS, greet_domain, 0)
    lax.fori_loop(1, REGIONS, greet_region, 0)

    pairs_in = zip((mid_in, lin_in, bur_in, dest_in, nid_in, cid_in, cen_in), (mid, lin, bur, dest, nid, cid, cen))
    loads = [pltpu.make_async_copy(there, here, in_sem.at[n]) for n, (there, here) in enumerate(pairs_in)]
    for load in loads:
        load.start()

    def empty(*accs):
        for acc in accs:
            pltpu.matmul_pop(acc)

    pl.run_scoped(empty, *[pltpu.ACC(w)((SEG, TILE), F32) for w in range(2)])

    for load in loads:
        load.wait()

    middle = [(region.astype(F32) + 0.5) / REGIONS, 0.5, 0.5]
    m = [mid[a : a + 1, :] - middle[a] for a in range(3)]
    l, b = rows_of(lin), rows_of(bur)
    for c, row in enumerate(m + l + b):
        for j in range(4):
            geo[0, 4 * c + j : 4 * c + j + 1, :] = row[:, j * LANES : (j + 1) * LANES]
    for j in range(4):
        geo[0, 36 + j : 37 + j, :] = jnp.zeros((1, LANES), F32)

    outer = [b[i] * l[j] for i in range(3) for j in range(3)]
    q = cross(b, l)
    zero = jnp.zeros((1, SEG), F32)
    feats = outer + [outer[k] * m[a] for a in range(3) for k in range(9)]
    feats = jnp.concatenate(feats + q + [zero], axis=0)
    cell_hot = (lax.broadcasted_iota(I32, (LANES, SEG), 0) == cid[...]).astype(F32).astype(BF16)
    feats = [jnp.concatenate([part, jnp.zeros((8, SEG), BF16)], axis=0) for part in split3(feats)]
    parts = dot_nt(jnp.concatenate(feats, axis=0), cell_hot)[:, 0:LANES]
    mom[...] = parts[0:40] + parts[48:88] + parts[96:136]

    def y_copy(k):
        return pltpu.make_async_remote_copy(
            src_ref=mom, dst_ref=my_in.at[k], send_sem=my_send.at[k], recv_sem=my_recv.at[k],
            device_id=(region, z * NY + (y + k) % NY), device_id_type=MESH)

    def geo_copy(source, k, peer):
        return pltpu.make_async_remote_copy(
            src_ref=geo.at[source], dst_ref=geo.at[k], send_sem=geo_send.at[k], recv_sem=geo_recv.at[k],
            device_id=(region, peer), device_id_type=MESH)

    def geo_along_z(i):
        return geo_copy(0, i, ((z + z_offset(i)) % NZ) * NY + y)

    def geo_along_y(source, step):
        return geo_copy(source, NZ + (NY - 1) * source + step - 1, z * NY + (y + step) % NY)

    def pass_on(source):
        for step in range(1, NY):
            geo_along_y(source, step).start()

    def z_copy(k):
        return pltpu.make_async_remote_copy(
            src_ref=mz_in.at[0], dst_ref=mz_in.at[k], send_sem=mz_send.at[k], recv_sem=mz_recv.at[k],
            device_id=(region, ((z + k) % NZ) * NY + y), device_id_type=MESH)

    def r_copy(k):
        return pltpu.make_async_remote_copy(
            src_ref=mall.at[0], dst_ref=mall.at[k], send_sem=mr_send.at[k], recv_sem=mr_recv.at[k],
            device_id=((region + k) % REGIONS, dom), device_id_type=MESH)

    def geo_wait(k):
        return geo_copy(0, k, z * NY + (y + 1) % NY)

    def start(copy):
        def run(k, c):
            copy(k).start()
            return c

        return run

    d = dest[...]
    hot = (lax.broadcasted_iota(I32, (DOMAINS, SEG), 0) == d).astype(F32)
    upper = lax.broadcasted_iota(I32, (TILE, TILE), 0) < lax.broadcasted_iota(I32, (TILE, TILE), 1)
    upper = upper.astype(F32).astype(BF16)
    first, second = hot[:, 0:TILE].astype(BF16), hot[:, TILE:SEG].astype(BF16)
    ones = jnp.ones((TILE, TILE), BF16)
    before = jnp.concatenate(
        [mxu_sum(DOMAINS, [(first, upper, False)]), mxu_sum(DOMAINS, [(second, upper, False), (first, ones, False)])], axis=1
    )
    rank = jnp.sum(before * hot, axis=0, keepdims=True)
    desthot[...] = hot
    rankhot[...] = (lax.broadcasted_iota(I32, (DOMAINS, SEG), 0).astype(F32) == rank).astype(F32).astype(BF16)
    for e in range(2):
        low = nid[e : e + 1, :] & (LANES - 1)
        nodehot[:, e * SEG : (e + 1) * SEG] = (lax.broadcasted_iota(I32, (LANES, SEG), 0) == low).astype(F32).astype(BF16)

    own = jnp.concatenate([-2.0 * m[a] for a in range(3)] + [m[0] * m[0] + m[1] * m[1] + m[2] * m[2] + CORE2] + [zero] * 4, axis=0)
    columns = jnp.transpose(own)
    for a in range(4):
        xb[a] = jnp.broadcast_to(columns[:, a : a + 1], (SEG, LANES))
    wsc[...] = jnp.zeros_like(wsc)

    at = pl.ds(pl.multiple_of(region * LANES, LANES), LANES)
    target = jnp.transpose(jnp.concatenate([cen[0:3, at], jnp.zeros((5, LANES), F32)], axis=0))
    target = [jnp.broadcast_to(target[:, a : a + 1], (LANES, LANES)) for a in range(3)]
    for k in range(1, REGIONS):
        source = pl.ds(pl.multiple_of(((region + REGIONS - k) % REGIONS) * LANES, LANES), LANES)
        diff = [target[a] - cen[a : a + 1, source] for a in range(3)]
        g1 = lax.rsqrt(diff[0] * diff[0] + diff[1] * diff[1] + diff[2] * diff[2] + CORE2)
        g3 = g1 * g1 * g1
        for p, part in enumerate([g1] + [diff[a] * g3 for a in range(3)]):
            kern[4 * (k - 1) + p] = jnp.concatenate(split2(part), axis=1)

    def pairs(*accs):
        acc1, acc3 = accs[:CHUNKS], accs[CHUNKS:]
        blank = jnp.zeros((TILE - 32, TILE), BF16)

        def prepare(k, slot):
            v = [geo[k, 4 * c : 4 * c + 4, :] for c in range(9)]
            vm, vl, vb = v[0:3], v[3:6], v[6:9]
            vq = cross(vb, vl)
            for i in range(3):
                for j in range(3):
                    at = 4 * (3 * i + j)
                    wsc[slot, 0, at : at + 4, :] = vb[i] * vl[j]
                    wsc[slot, 1, at : at + 4, :] = vq[i] * vm[j]
                wsc[slot, 1, 36 + 4 * i : 40 + 4 * i, :] = vq[i]

        def push(slot, t):
            for w in range(2):
                wide = jnp.concatenate([wsc[slot, w, pl.ds(2 * t + u, 16, stride=4), :] for u in range(2)], axis=1)
                high, low = split2(wide)
                pltpu.matmul_push_rhs(jnp.concatenate([high, low, blank] if w == 0 else [blank[0:32], high, low, blank[32:]], axis=0), t, w, transpose=True)

        def stream(k, t):
            s = [
                jnp.concatenate([geo[k, 4 * a + 2 * t + u : 4 * a + 2 * t + u + 1, :] for u in range(2)], axis=1)
                for a in range(3)
            ]
            s2 = s[0] * s[0] + s[1] * s[1] + s[2] * s[2]
            for c in range(CHUNKS):
                x = [jnp.concatenate([xb[a, c * CHUNK : (c + 1) * CHUNK, :]] * 2, axis=1) for a in range(4)]
                g1 = lax.rsqrt((x[3] + s2) + x[0] * s[0] + x[1] * s[1] + x[2] * s[2])
                h1, l1 = split2(g1)
                h3, l3 = split2(g1 * g1 * g1)
                first = t if c == 0 else None
                pltpu.matmul_acc_lhs(acc1[c], h1, first)
                pltpu.matmul_acc_lhs(acc3[c], h3, first)
                pltpu.matmul_acc_lhs(acc1[c], l1)
                pltpu.matmul_acc_lhs(acc3[c], l3)

        def column_moments():
            for k in range(1, NY):
                y_copy(k).wait_recv()
            mz_in[0] = mom[...] + my_in[1] + my_in[2] + my_in[3]
            for k in range(1, NZ):
                z_copy(k).start()

        def region_moments():
            for k in range(1, NZ):
                z_copy(k).wait_recv()
            total = mz_in[0]
            for k in range(1, NZ):
                total = total + mz_in[k]
            center = [cen[a : a + 1, pl.ds(pl.multiple_of(region * LANES, LANES), LANES)] - middle[a] for a in range(3)]
            mall[0, 0:9, :] = total[0:9]
            for a in range(3):
                for k in range(9):
                    at = 9 + 9 * a + k
                    value = total[at : at + 1] - center[a] * total[k : k + 1]
                    if k % 3 == a:
                        value = value + total[36 + k // 3 : 37 + k // 3]
                    mall[0, at : at + 1, :] = value
            mall[0, 36:40, :] = jnp.zeros((4, LANES), F32)
            for k in range(1, REGIONS):
                r_copy(k).start()

        def block(k, carry):
            push(k % 2, 1)
            stream(k, 0)
            later = (k + 1) - (k + 1) // DOMAINS

            @pl.when(k < DOMAINS - 1)
            def _():
                geo_wait(later).wait_recv()

            @pl.when(k < NZ - 1)
            def _():
                pass_on(later)

            @pl.when(k == NZ - 2)
            def _():
                column_moments()

            @pl.when(k == 15)
            def _():
                region_moments()

            prepare(later, (k + 1) % 2)
            push((k + 1) % 2, 0)
            stream(k, 1)
            return carry

        prepare(0, 0)
        push(0, 0)
        push(0, 1)
        stream(0, 0)
        stream(0, 1)

        pl.semaphore_wait(barrier, DOMAINS - 1 + REGIONS - 1)
        lax.fori_loop(1, NZ, start(geo_along_z), 0)
        for k in range(1, NY):
            y_copy(k).start()
        pass_on(0)
        geo_wait(1).wait_recv()
        pass_on(1)
        prepare(1, 1)
        push(1, 0)
        lax.fori_loop(1, DOMAINS, block, 0)
        pltpu.matmul_acc_lhs(acc1[0], jnp.zeros((CHUNK, TILE), BF16), 0)
        pltpu.matmul_acc_lhs(acc3[0], jnp.zeros((CHUNK, TILE), BF16), 0)
        for c in range(CHUNKS):
            one, three = pltpu.matmul_pop(acc1[c]), pltpu.matmul_pop(acc3[c])
            xb[0, c * CHUNK : (c + 1) * CHUNK, :] = one[:, 0:LANES] + three[:, 0:LANES]

    pl.run_scoped(pairs, *[pltpu.ACC(w)((CHUNK, TILE), F32) for w in range(2) for _ in range(CHUNKS)])

    for k in range(1, REGIONS):
        r_copy(k).wait_recv()
    steps = []
    for k in range(1, REGIONS):
        total = mall[k]
        for p in range(4):
            wh, wl = split2(jnp.concatenate([total[9 * p : 9 * p + 9], jnp.zeros((7, LANES), F32)], axis=0))
            both = jnp.concatenate([wh, wl], axis=0)
            steps.append((jnp.concatenate([both, both], axis=1), padded(kern[4 * (k - 1) + p]), True))
    far = mxu_sum(32, steps)
    far = split3(far[0:16, 0:LANES] + far[16:32, 0:LANES])
    cell_hot = (lax.broadcasted_iota(I32, (TILE, SEG), 0) % LANES == cid[...]).astype(F32).astype(BF16)
    pair = [jnp.concatenate(far[0:2], axis=1), jnp.concatenate([far[2], jnp.zeros_like(far[2])], axis=1)]
    far = jnp.concatenate(
        [mxu_sum(16, [(left, cell_hot[:, k : k + TILE], False) for left in pair]) for k in (0, TILE)], axis=1
    )

    sums = jnp.transpose(xb[0])
    one, three = sums[0:16] + sums[16:32], sums[32:48] + sums[48:64]
    x = [mid[a : a + 1, :] - middle[a] for a in range(3)]
    b = rows_of(bur)
    stress = [
        one[k : k + 1] + far[k : k + 1] + three[9 + k // 3 : 10 + k // 3] * x[k % 3] - three[k : k + 1] for k in range(9)
    ]
    force = []
    for i in range(3):
        total = zero
        for j in range(3):
            total = total + 0.5 * (stress[3 * i + j] + stress[3 * j + i]) * b[j]
        force.append(total)

    halves = [0.5 * f for f in force]
    table = jnp.concatenate([halves[0]] * 2 + [halves[1]] * 2 + [halves[2]] * 2 + [zero] * 2, axis=0)
    table_high = table.astype(BF16).astype(F32)
    table_low = table - table_high
    sub = lax.broadcasted_iota(I32, (8, SEG), 0) % 2
    lefts = []
    for e in range(2):
        row = (nid[e : e + 1, :] // LANES) - sub
        hits = [row == 2 * owner for owner in range(DOMAINS)]
        for part in (table_high, table_low):
            lefts.append(jnp.concatenate([jnp.where(hit, part, 0.0) for hit in hits], axis=0).astype(BF16))
    rights = [nodehot[:, e * SEG : (e + 1) * SEG] for e in (0, 0, 1, 1)]
    nodes = dot_nt(jnp.concatenate(lefts, axis=1), jnp.concatenate(rights, axis=1))
    hot = desthot[...]
    left = [part for c in range(3) for part in split3(hot * force[c])]
    part = dot_nt(jnp.concatenate(left, axis=0), rankhot[...])[:, 0:32]
    slots = [part[96 * c : 96 * c + 32] + part[96 * c + 32 : 96 * c + 64] + part[96 * c + 64 : 96 * c + 96] for c in range(3)]
    slots = jnp.concatenate(slots + [jnp.zeros((DOMAINS, 32), F32)], axis=1)
    msg[...] = nodes[:, 0:LANES]
    msg[pl.ds(6, DOMAINS, stride=8), :] = slots

    def out_copy(k):
        peer = (dom + DOMAINS // 2 + (k % 2) * (k // 2) + (1 - k % 2) * (DOMAINS - k // 2)) % DOMAINS
        return pltpu.make_async_remote_copy(
            src_ref=msg.at[pl.ds(pl.multiple_of(8 * peer, 8), 8), :],
            dst_ref=arrived.at[pl.ds(pl.multiple_of(8 * dom, 8), 8), :],
            send_sem=out_send.at[k], recv_sem=out_recv.at[k],
            device_id=(region, peer), device_id_type=MESH)

    lax.fori_loop(1, DOMAINS, start(out_copy), 0)
    mine = pl.ds(pl.multiple_of(8 * dom, 8), 8)
    arrived[mine, :] = msg[mine, :]

    def received(k, c):
        out_copy(k).wait_recv()
        return c

    lax.fori_loop(1, DOMAINS, received, 0)
    total = arrived[0:8, :]
    for s in range(1, DOMAINS):
        total = total + arrived[8 * s : 8 * s + 8, :]
    for c in range(3):
        for h in range(2):
            node_out[c : c + 1, h * LANES : (h + 1) * LANES] = total[2 * c + h : 2 * c + h + 1]
    quarter = lax.broadcasted_iota(I32, (8, LANES), 1) // 32
    four = [arrived[pl.ds(6 + 8 * a, 8, stride=32), :] for a in range(4)]
    for c in range(3):
        line = jnp.zeros((8, LANES), F32)
        for a in range(4):
            turn = (32 * (a - c)) % LANES
            line = jnp.where(quarter == a, pltpu.roll(four[a], turn, 1) if turn else four[a], line)
        for j in range(8):
            slot_out[c : c + 1, j * LANES : (j + 1) * LANES] = line[j : j + 1]

    for copy, count in ((y_copy, NY), (geo_wait, DOMAINS), (z_copy, NZ), (r_copy, REGIONS), (out_copy, DOMAINS)):

        def sent(k, c, copy=copy):
            copy(k).wait_send()
            return c

        lax.fori_loop(1, count, sent, 0)


def body(midpoints, line_vectors, burgers, destination, node_ids, cell_ids, cell_centers):
    vmem = pl.BlockSpec(memory_space=pltpu.VMEM)
    dma = pltpu.SemaphoreType.DMA
    inputs = (midpoints, line_vectors, burgers, destination.reshape(1, SEG), node_ids, cell_ids.reshape(1, SEG), cell_centers)
    inputs = [pltpu.with_memory_space_constraint(value, pltpu.HBM) for value in inputs]
    return pl.pallas_call(
        kernel,
        out_shape=(jax.ShapeDtypeStruct((3, 2 * SEG), F32), jax.ShapeDtypeStruct((3, 256), F32)),
        in_specs=[pl.BlockSpec(memory_space=pltpu.HBM)] * 7,
        out_specs=(vmem, vmem),
        scratch_shapes=[
            pltpu.VMEM((3, SEG), F32),
            pltpu.VMEM((3, SEG), F32),
            pltpu.VMEM((3, SEG), F32),
            pltpu.VMEM((1, SEG), I32),
            pltpu.VMEM((2, SEG), I32),
            pltpu.VMEM((1, SEG), I32),
            pltpu.VMEM((3, REGIONS * LANES), F32),
            dma((7,)),
            pltpu.VMEM((4 * (REGIONS - 1), LANES, TILE), BF16),
            pltpu.VMEM((DOMAINS, 40, LANES), F32),
            pltpu.VMEM((4, SEG, LANES), F32),
            pltpu.VMEM((2, 2, 64, LANES), F32),
            pltpu.VMEM((40, LANES), F32),
            pltpu.VMEM((NY, 40, LANES), F32),
            pltpu.VMEM((NZ, 40, LANES), F32),
            pltpu.VMEM((REGIONS, 40, LANES), F32),
            pltpu.VMEM((DOMAINS * 8, LANES), F32),
            pltpu.VMEM((DOMAINS * 8, LANES), F32),
            pltpu.VMEM((LANES, 2 * SEG), BF16),
            pltpu.VMEM((DOMAINS, SEG), BF16),
            pltpu.VMEM((DOMAINS, SEG), F32),
            dma((DOMAINS,)), dma((DOMAINS,)), dma((NY,)), dma((NY,)), dma((NZ,)), dma((NZ,)),
            dma((REGIONS,)), dma((REGIONS,)), dma((DOMAINS,)), dma((DOMAINS,)),
        ],
        compiler_params=pltpu.CompilerParams(
            collective_id=0, has_side_effects=True, vmem_limit_bytes=32 << 20
        ),
    )(*inputs)


def solution(mesh):
    both = ("region", "domain")

    def program(*args):
        with jax.sharding.use_abstract_mesh(mesh.abstract_mesh):
            return jax.shard_map(
                body,
                mesh=mesh,
                in_specs=(P(None, both), P(None, both), P(None, both), P(both, None), P(None, both), P(both), P()),
                out_specs=(P(None, both), P(None, both)),
                check_vma=False,
            )(*args)

    return program
```

```python
import jax
import jax.numpy as jnp
from jax import lax
from jax.experimental import pallas as pl
from jax.experimental.pallas import tpu as pltpu
from jax.sharding import PartitionSpec as P

MESH = pl.DeviceIdType.MESH
F32, BF16, I32 = jnp.float32, jnp.bfloat16, jnp.int32
CORE2 = 0.01
REGIONS, DOMAINS, NZ, NY = 8, 32, 8, 4
SEG, TILE, CHUNK, LANES = 512, 256, 64, 128
CHUNKS = SEG // CHUNK


def split2(v):
    high = v.astype(BF16)
    return high, (v - high.astype(F32)).astype(BF16)


def split3(v):
    high = v.astype(BF16)
    rest = v - high.astype(F32)
    mid = rest.astype(BF16)
    return high, mid, (rest - mid.astype(F32)).astype(BF16)


def cross(b, l):
    return [b[1] * l[2] - b[2] * l[1], b[2] * l[0] - b[0] * l[2], b[0] * l[1] - b[1] * l[0]]


def rows_of(ref):
    return [ref[a : a + 1, :] for a in range(3)]


def mxu_sum(rows, steps):
    def run(*accs):
        for n, (left, right, turned) in enumerate(steps):
            unit, stage = n % 2, n // 2 % 2
            pltpu.matmul_push_rhs(right, stage, unit, transpose=turned)
            pltpu.matmul_acc_lhs(accs[unit], left, stage)
        total = pltpu.matmul_pop(accs[0])
        return total + pltpu.matmul_pop(accs[1]) if len(steps) > 1 else total

    return pl.run_scoped(run, *[pltpu.ACC(w)((rows, TILE), F32) for w in range(2)])


def padded(right):
    return jnp.concatenate([right, jnp.zeros((TILE - right.shape[0], right.shape[1]), right.dtype)], axis=0)


def dot_nt(left, right):
    tiles = [slice(k, k + TILE) for k in range(0, left.shape[1], TILE)]
    return mxu_sum(left.shape[0], [(left[:, k], padded(right[:, k]), True) for k in tiles])


def z_offset(i):
    odd = i % 2
    return odd * ((i + 1) // 2) + (1 - odd) * ((NZ - i // 2) % NZ)


def kernel(
    mid_in, lin_in, bur_in, dest_in, nid_in, cid_in, cen_in,
    slot_out, node_out,
    mid, lin, bur, dest, nid, cid, cen, in_sem, kern,
    geo, xb, wsc, mom, my_in, mz_in, mall, msg, arrived, nodehot, rankhot, desthot,
    geo_send, geo_recv, my_send, my_recv, mz_send, mz_recv, mr_send, mr_recv, out_send, out_recv,
):
    region, dom = lax.axis_index("region"), lax.axis_index("domain")
    z, y = dom // NY, dom % NY

    barrier = pltpu.get_barrier_semaphore()

    def greet_domain(k, c):
        pl.semaphore_signal(barrier, inc=1, device_id=(region, (dom + k) % DOMAINS), device_id_type=MESH)
        return c

    def greet_region(k, c):
        pl.semaphore_signal(barrier, inc=1, device_id=((region + k) % REGIONS, dom), device_id_type=MESH)
        return c

    lax.fori_loop(1, DOMAINS, greet_domain, 0)
    lax.fori_loop(1, REGIONS, greet_region, 0)

    pairs_in = zip((mid_in, lin_in, bur_in, dest_in, nid_in, cid_in, cen_in), (mid, lin, bur, dest, nid, cid, cen))
    loads = [pltpu.make_async_copy(there, here, in_sem.at[n]) for n, (there, here) in enumerate(pairs_in)]
    for load in loads:
        load.start()

    def empty(*accs):
        for acc in accs:
            pltpu.matmul_pop(acc)

    pl.run_scoped(empty, *[pltpu.ACC(w)((SEG, TILE), F32) for w in range(2)])

    for load in loads:
        load.wait()

    middle = [(region.astype(F32) + 0.5) / REGIONS, 0.5, 0.5]
    m = [mid[a : a + 1, :] - middle[a] for a in range(3)]
    l, b = rows_of(lin), rows_of(bur)
    for c, row in enumerate(m + l + b):
        for j in range(4):
            geo[0, 4 * c + j : 4 * c + j + 1, :] = row[:, j * LANES : (j + 1) * LANES]
    for j in range(4):
        geo[0, 36 + j : 37 + j, :] = jnp.zeros((1, LANES), F32)

    outer = [b[i] * l[j] for i in range(3) for j in range(3)]
    q = cross(b, l)
    zero = jnp.zeros((1, SEG), F32)
    feats = outer + [outer[k] * m[a] for a in range(3) for k in range(9)]
    feats = jnp.concatenate(feats + q + [zero], axis=0)
    cell_hot = (lax.broadcasted_iota(I32, (LANES, SEG), 0) == cid[...]).astype(F32).astype(BF16)
    feats = [jnp.concatenate([part, jnp.zeros((8, SEG), BF16)], axis=0) for part in split3(feats)]
    parts = dot_nt(jnp.concatenate(feats, axis=0), cell_hot)[:, 0:LANES]
    mom[...] = parts[0:40] + parts[48:88] + parts[96:136]

    def y_copy(k):
        return pltpu.make_async_remote_copy(
            src_ref=mom, dst_ref=my_in.at[k], send_sem=my_send.at[k], recv_sem=my_recv.at[k],
            device_id=(region, z * NY + (y + k) % NY), device_id_type=MESH)

    def geo_copy(source, k, peer):
        return pltpu.make_async_remote_copy(
            src_ref=geo.at[source], dst_ref=geo.at[k], send_sem=geo_send.at[k], recv_sem=geo_recv.at[k],
            device_id=(region, peer), device_id_type=MESH)

    def geo_along_z(i):
        return geo_copy(0, i, ((z + z_offset(i)) % NZ) * NY + y)

    def geo_along_y(source, step):
        return geo_copy(source, NZ + (NY - 1) * source + step - 1, z * NY + (y + step) % NY)

    def pass_on(source):
        for step in range(1, NY):
            geo_along_y(source, step).start()

    def z_copy(k):
        return pltpu.make_async_remote_copy(
            src_ref=mz_in.at[0], dst_ref=mz_in.at[k], send_sem=mz_send.at[k], recv_sem=mz_recv.at[k],
            device_id=(region, ((z + k) % NZ) * NY + y), device_id_type=MESH)

    def r_copy(k):
        return pltpu.make_async_remote_copy(
            src_ref=mall.at[0], dst_ref=mall.at[k], send_sem=mr_send.at[k], recv_sem=mr_recv.at[k],
            device_id=((region + k) % REGIONS, dom), device_id_type=MESH)

    def geo_wait(k):
        return geo_copy(0, k, z * NY + (y + 1) % NY)

    def start(copy):
        def run(k, c):
            copy(k).start()
            return c

        return run

    d = dest[...]
    hot = (lax.broadcasted_iota(I32, (DOMAINS, SEG), 0) == d).astype(F32)
    upper = lax.broadcasted_iota(I32, (TILE, TILE), 0) < lax.broadcasted_iota(I32, (TILE, TILE), 1)
    upper = upper.astype(F32).astype(BF16)
    first, second = hot[:, 0:TILE].astype(BF16), hot[:, TILE:SEG].astype(BF16)
    ones = jnp.ones((TILE, TILE), BF16)
    before = jnp.concatenate(
        [mxu_sum(DOMAINS, [(first, upper, False)]), mxu_sum(DOMAINS, [(second, upper, False), (first, ones, False)])], axis=1
    )
    rank = jnp.sum(before * hot, axis=0, keepdims=True)
    desthot[...] = hot
    rankhot[...] = (lax.broadcasted_iota(I32, (DOMAINS, SEG), 0).astype(F32) == rank).astype(F32).astype(BF16)
    for e in range(2):
        low = nid[e : e + 1, :] & (LANES - 1)
        nodehot[:, e * SEG : (e + 1) * SEG] = (lax.broadcasted_iota(I32, (LANES, SEG), 0) == low).astype(F32).astype(BF16)

    own = jnp.concatenate([-2.0 * m[a] for a in range(3)] + [m[0] * m[0] + m[1] * m[1] + m[2] * m[2] + CORE2] + [zero] * 4, axis=0)
    columns = jnp.transpose(own)
    for a in range(4):
        xb[a] = jnp.broadcast_to(columns[:, a : a + 1], (SEG, LANES))
    wsc[...] = jnp.zeros_like(wsc)

    at = pl.ds(pl.multiple_of(region * LANES, LANES), LANES)
    target = jnp.transpose(jnp.concatenate([cen[0:3, at], jnp.zeros((5, LANES), F32)], axis=0))
    target = [jnp.broadcast_to(target[:, a : a + 1], (LANES, LANES)) for a in range(3)]
    for k in range(1, REGIONS):
        source = pl.ds(pl.multiple_of(((region + REGIONS - k) % REGIONS) * LANES, LANES), LANES)
        diff = [target[a] - cen[a : a + 1, source] for a in range(3)]
        g1 = lax.rsqrt(diff[0] * diff[0] + diff[1] * diff[1] + diff[2] * diff[2] + CORE2)
        g3 = g1 * g1 * g1
        for p, part in enumerate([g1] + [diff[a] * g3 for a in range(3)]):
            kern[4 * (k - 1) + p] = jnp.concatenate(split2(part), axis=1)

    def pairs(*accs):
        acc1, acc3 = accs[:CHUNKS], accs[CHUNKS:]
        blank = jnp.zeros((TILE - 32, TILE), BF16)

        def prepare(k, slot):
            v = [geo[k, 4 * c : 4 * c + 4, :] for c in range(9)]
            vm, vl, vb = v[0:3], v[3:6], v[6:9]
            vq = cross(vb, vl)
            for i in range(3):
                for j in range(3):
                    at = 4 * (3 * i + j)
                    wsc[slot, 0, at : at + 4, :] = vb[i] * vl[j]
                    wsc[slot, 1, at : at + 4, :] = vq[i] * vm[j]
                wsc[slot, 1, 36 + 4 * i : 40 + 4 * i, :] = vq[i]

        def push(slot, t):
            for w in range(2):
                wide = jnp.concatenate([wsc[slot, w, pl.ds(2 * t + u, 16, stride=4), :] for u in range(2)], axis=1)
                high, low = split2(wide)
                pltpu.matmul_push_rhs(jnp.concatenate([high, low, blank] if w == 0 else [blank[0:32], high, low, blank[32:]], axis=0), t, w, transpose=True)

        def stream(k, t):
            s = [
                jnp.concatenate([geo[k, 4 * a + 2 * t + u : 4 * a + 2 * t + u + 1, :] for u in range(2)], axis=1)
                for a in range(3)
            ]
            s2 = s[0] * s[0] + s[1] * s[1] + s[2] * s[2]
            for c in range(CHUNKS):
                x = [jnp.concatenate([xb[a, c * CHUNK : (c + 1) * CHUNK, :]] * 2, axis=1) for a in range(4)]
                g1 = lax.rsqrt((x[3] + s2) + x[0] * s[0] + x[1] * s[1] + x[2] * s[2])
                h1, l1 = split2(g1)
                h3, l3 = split2(g1 * g1 * g1)
                first = t if c == 0 else None
                pltpu.matmul_acc_lhs(acc1[c], h1, first)
                pltpu.matmul_acc_lhs(acc3[c], h3, first)
                pltpu.matmul_acc_lhs(acc1[c], l1)
                pltpu.matmul_acc_lhs(acc3[c], l3)

        def column_moments():
            for k in range(1, NY):
                y_copy(k).wait_recv()
            mz_in[0] = mom[...] + my_in[1] + my_in[2] + my_in[3]
            for k in range(1, NZ):
                z_copy(k).start()

        def region_moments():
            for k in range(1, NZ):
                z_copy(k).wait_recv()
            total = mz_in[0]
            for k in range(1, NZ):
                total = total + mz_in[k]
            center = [cen[a : a + 1, pl.ds(pl.multiple_of(region * LANES, LANES), LANES)] - middle[a] for a in range(3)]
            mall[0, 0:9, :] = total[0:9]
            for a in range(3):
                for k in range(9):
                    at = 9 + 9 * a + k
                    value = total[at : at + 1] - center[a] * total[k : k + 1]
                    if k % 3 == a:
                        value = value + total[36 + k // 3 : 37 + k // 3]
                    mall[0, at : at + 1, :] = value
            mall[0, 36:40, :] = jnp.zeros((4, LANES), F32)
            for k in range(1, REGIONS):
                r_copy(k).start()

        def block(k, carry):
            push(k % 2, 1)
            stream(k, 0)
            later = (k + 1) - (k + 1) // DOMAINS

            @pl.when(k < DOMAINS - 1)
            def _():
                geo_wait(later).wait_recv()

            @pl.when(k < NZ - 1)
            def _():
                pass_on(later)

            @pl.when(k == NZ - 2)
            def _():
                column_moments()

            @pl.when(k == 15)
            def _():
                region_moments()

            prepare(later, (k + 1) % 2)
            push((k + 1) % 2, 0)
            stream(k, 1)
            return carry

        prepare(0, 0)
        push(0, 0)
        push(0, 1)
        stream(0, 0)
        stream(0, 1)

        pl.semaphore_wait(barrier, DOMAINS - 1 + REGIONS - 1)
        lax.fori_loop(1, NZ, start(geo_along_z), 0)
        for k in range(1, NY):
            y_copy(k).start()
        pass_on(0)
        geo_wait(1).wait_recv()
        pass_on(1)
        prepare(1, 1)
        push(1, 0)
        lax.fori_loop(1, DOMAINS, block, 0)
        pltpu.matmul_acc_lhs(acc1[0], jnp.zeros((CHUNK, TILE), BF16), 0)
        pltpu.matmul_acc_lhs(acc3[0], jnp.zeros((CHUNK, TILE), BF16), 0)
        for c in range(CHUNKS):
            one, three = pltpu.matmul_pop(acc1[c]), pltpu.matmul_pop(acc3[c])
            xb[0, c * CHUNK : (c + 1) * CHUNK, :] = one[:, 0:LANES] + three[:, 0:LANES]

    pl.run_scoped(pairs, *[pltpu.ACC(w)((CHUNK, TILE), F32) for w in range(2) for _ in range(CHUNKS)])

    for k in range(1, REGIONS):
        r_copy(k).wait_recv()
    steps = []
    for k in range(1, REGIONS):
        total = mall[k]
        for p in range(4):
            wh, wl = split2(jnp.concatenate([total[9 * p : 9 * p + 9], jnp.zeros((7, LANES), F32)], axis=0))
            both = jnp.concatenate([wh, wl], axis=0)
            steps.append((jnp.concatenate([both, both], axis=1), padded(kern[4 * (k - 1) + p]), True))
    far = mxu_sum(32, steps)
    far = split3(far[0:16, 0:LANES] + far[16:32, 0:LANES])
    cell_hot = (lax.broadcasted_iota(I32, (TILE, SEG), 0) % LANES == cid[...]).astype(F32).astype(BF16)
    pair = [jnp.concatenate(far[0:2], axis=1), jnp.concatenate([far[2], jnp.zeros_like(far[2])], axis=1)]
    far = jnp.concatenate(
        [mxu_sum(16, [(left, cell_hot[:, k : k + TILE], False) for left in pair]) for k in (0, TILE)], axis=1
    )

    sums = jnp.transpose(xb[0])
    one, three = sums[0:16] + sums[16:32], sums[32:48] + sums[48:64]
    x = [mid[a : a + 1, :] - middle[a] for a in range(3)]
    b = rows_of(bur)
    stress = [
        one[k : k + 1] + far[k : k + 1] + three[9 + k // 3 : 10 + k // 3] * x[k % 3] - three[k : k + 1] for k in range(9)
    ]
    force = []
    for i in range(3):
        total = zero
        for j in range(3):
            total = total + 0.5 * (stress[3 * i + j] + stress[3 * j + i]) * b[j]
        force.append(total)

    halves = [0.5 * f for f in force]
    table = jnp.concatenate([halves[0]] * 2 + [halves[1]] * 2 + [halves[2]] * 2 + [zero] * 2, axis=0)
    table_high = table.astype(BF16).astype(F32)
    table_low = table - table_high
    sub = lax.broadcasted_iota(I32, (8, SEG), 0) % 2
    lefts = []
    for e in range(2):
        row = (nid[e : e + 1, :] // LANES) - sub
        hits = [row == 2 * owner for owner in range(DOMAINS)]
        for part in (table_high, table_low):
            lefts.append(jnp.concatenate([jnp.where(hit, part, 0.0) for hit in hits], axis=0).astype(BF16))
    rights = [nodehot[:, e * SEG : (e + 1) * SEG] for e in (0, 0, 1, 1)]
    nodes = dot_nt(jnp.concatenate(lefts, axis=1), jnp.concatenate(rights, axis=1))
    hot = desthot[...]
    left = [part for c in range(3) for part in split3(hot * force[c])]
    part = dot_nt(jnp.concatenate(left, axis=0), rankhot[...])[:, 0:32]
    slots = [part[96 * c : 96 * c + 32] + part[96 * c + 32 : 96 * c + 64] + part[96 * c + 64 : 96 * c + 96] for c in range(3)]
    slots = jnp.concatenate(slots + [jnp.zeros((DOMAINS, 32), F32)], axis=1)
    msg[...] = nodes[:, 0:LANES]
    msg[pl.ds(6, DOMAINS, stride=8), :] = slots

    def out_copy(k):
        peer = (dom + DOMAINS // 2 + (k % 2) * (k // 2) + (1 - k % 2) * (DOMAINS - k // 2)) % DOMAINS
        return pltpu.make_async_remote_copy(
            src_ref=msg.at[pl.ds(pl.multiple_of(8 * peer, 8), 8), :],
            dst_ref=arrived.at[pl.ds(pl.multiple_of(8 * dom, 8), 8), :],
            send_sem=out_send.at[k], recv_sem=out_recv.at[k],
            device_id=(region, peer), device_id_type=MESH)

    lax.fori_loop(1, DOMAINS, start(out_copy), 0)
    mine = pl.ds(pl.multiple_of(8 * dom, 8), 8)
    arrived[mine, :] = msg[mine, :]

    for copy, count in ((y_copy, NY), (geo_wait, DOMAINS), (z_copy, NZ), (r_copy, REGIONS), (out_copy, DOMAINS)):

        def sent(k, c, copy=copy):
            copy(k).wait_send()
            return c

        lax.fori_loop(1, count, sent, 0)

    def received(k, c):
        out_copy(k).wait_recv()
        return c

    lax.fori_loop(1, DOMAINS, received, 0)
    total = arrived[0:8, :]
    for s in range(1, DOMAINS):
        total = total + arrived[8 * s : 8 * s + 8, :]
    for c in range(3):
        for h in range(2):
            node_out[c : c + 1, h * LANES : (h + 1) * LANES] = total[2 * c + h : 2 * c + h + 1]
    quarter = lax.broadcasted_iota(I32, (8, LANES), 1) // 32
    four = [arrived[pl.ds(6 + 8 * a, 8, stride=32), :] for a in range(4)]
    for c in range(3):
        line = jnp.zeros((8, LANES), F32)
        for a in range(4):
            turn = (32 * (a - c)) % LANES
            line = jnp.where(quarter == a, pltpu.roll(four[a], turn, 1) if turn else four[a], line)
        for j in range(8):
            slot_out[c : c + 1, j * LANES : (j + 1) * LANES] = line[j : j + 1]


def body(midpoints, line_vectors, burgers, destination, node_ids, cell_ids, cell_centers):
    vmem = pl.BlockSpec(memory_space=pltpu.VMEM)
    dma = pltpu.SemaphoreType.DMA
    inputs = (midpoints, line_vectors, burgers, destination.reshape(1, SEG), node_ids, cell_ids.reshape(1, SEG), cell_centers)
    inputs = [pltpu.with_memory_space_constraint(value, pltpu.HBM) for value in inputs]
    return pl.pallas_call(
        kernel,
        out_shape=(jax.ShapeDtypeStruct((3, 2 * SEG), F32), jax.ShapeDtypeStruct((3, 256), F32)),
        in_specs=[pl.BlockSpec(memory_space=pltpu.HBM)] * 7,
        out_specs=(vmem, vmem),
        scratch_shapes=[
            pltpu.VMEM((3, SEG), F32),
            pltpu.VMEM((3, SEG), F32),
            pltpu.VMEM((3, SEG), F32),
            pltpu.VMEM((1, SEG), I32),
            pltpu.VMEM((2, SEG), I32),
            pltpu.VMEM((1, SEG), I32),
            pltpu.VMEM((3, REGIONS * LANES), F32),
            dma((7,)),
            pltpu.VMEM((4 * (REGIONS - 1), LANES, TILE), BF16),
            pltpu.VMEM((DOMAINS, 40, LANES), F32),
            pltpu.VMEM((4, SEG, LANES), F32),
            pltpu.VMEM((2, 2, 64, LANES), F32),
            pltpu.VMEM((40, LANES), F32),
            pltpu.VMEM((NY, 40, LANES), F32),
            pltpu.VMEM((NZ, 40, LANES), F32),
            pltpu.VMEM((REGIONS, 40, LANES), F32),
            pltpu.VMEM((DOMAINS * 8, LANES), F32),
            pltpu.VMEM((DOMAINS * 8, LANES), F32),
            pltpu.VMEM((LANES, 2 * SEG), BF16),
            pltpu.VMEM((DOMAINS, SEG), BF16),
            pltpu.VMEM((DOMAINS, SEG), F32),
            dma((DOMAINS,)), dma((DOMAINS,)), dma((NY,)), dma((NY,)), dma((NZ,)), dma((NZ,)),
            dma((REGIONS,)), dma((REGIONS,)), dma((DOMAINS,)), dma((DOMAINS,)),
        ],
        compiler_params=pltpu.CompilerParams(
            collective_id=0, has_side_effects=True, vmem_limit_bytes=32 << 20
        ),
    )(*inputs)


def solution(mesh):
    both = ("region", "domain")

    def program(*args):
        with jax.sharding.use_abstract_mesh(mesh.abstract_mesh):
            return jax.shard_map(
                body,
                mesh=mesh,
                in_specs=(P(None, both), P(None, both), P(None, both), P(both, None), P(None, both), P(both), P()),
                out_specs=(P(None, both), P(None, both)),
                check_vma=False,
            )(*args)

    return program
```
